32 devices in a mesh: sec: 8 (over z, x), blk: 4 (over y, core).
Axes of the slice: x: 2, y: 2, z: 4, core: 2. Of those that a mesh axis runs over, the one named last changes fastest.
Arguments:
- features: bfloat16 [8, 52, 8192], P('sec', None, 'blk'), may hold values from -6 to 6
- programs: bfloat16 [8, 32, 8192], P('sec', None, 'blk'), may hold values from -6 to 6
- column_pot: bfloat16 [8, 8192], P('sec', 'blk'), may hold values from -12 to 12
- tile_pairs: int32 [2, 8, 112], P(None, 'sec', 'blk'), may hold values from 0 to 15, as said below
- pair_counts: int32 [8, 4], P('sec', 'blk'), may hold values from 0 to 28, as said below
Outputs:
- smoothed: bfloat16 [8, 32, 8192], P('sec', None, 'blk')
- row_potential: float32 [8, 8192], P('sec', 'blk')
- column_potential: float32 [8, 8192], P('sec', 'blk')
The draws below stay inside these ranges and needn't reach their ends.
Inputs may be any that keep to these rules, and one draw needn't show every extreme that they name: `tile_pairs`: entry [0, s, b * 28 + k] is a row tile of block b of section s counted within the block (0 to 3); entry [1, s, b * 28 + k] is a tile of section s + 1 (0 to 15). Only slots k < pair_counts[s, b] are active; slots from there on hold in-range entries that do not count. The active pairs of one block are distinct; in every section but the last, every row tile of every block is in an active pair, and every tile of section s + 1 is in an active pair of section s. `pair_counts`: 0 in the last section; in every other section from 4 to 28, and one block of every such section holds exactly 28.
All inputs are finite; a program needn't handle non-finite values.
Results may differ from the reference program's by a relative error of at most 0.0034.
Values may be sent and summed in bfloat16 or wider, within the bound.
A program may use at most 64 MiB of HBM per device.

```python
import jax
import jax.numpy as jnp
from jax import lax

FEAT = 52
PROGS = 32
TILE = 512
TILES_BLK = 4
SECTIONS = 8
TILES_SEC = 16
CELLS = 8192
MAXP = 28
SLOTS = 112
N_BLK = 4


def pair_plan(key):
    dense = jax.random.randint(jax.random.fold_in(key, 11), (SECTIONS,), 0, N_BLK)
    lighter = jax.random.randint(jax.random.fold_in(key, 12), (SECTIONS, N_BLK), TILES_BLK, TILES_BLK + TILES_BLK // 2 + 1)
    block_ids = jnp.arange(N_BLK, dtype=jnp.int32)
    section_ids = jnp.arange(SECTIONS, dtype=jnp.int32)
    counts = jnp.where(block_ids[None, :] == dense[:, None], MAXP, lighter)
    counts = jnp.where(section_ids[:, None] == SECTIONS - 1, 0, counts).astype(jnp.int32)
    shift_keys = jax.random.split(jax.random.fold_in(key, 13), SECTIONS * N_BLK)
    offsets = jax.vmap(lambda one_key: jax.random.permutation(one_key, TILES_SEC - 1) + 1)(shift_keys)
    order_keys = jax.random.split(jax.random.fold_in(key, 14), SECTIONS * N_BLK)
    row_orders = jax.vmap(lambda one_key: jax.random.permutation(one_key, TILES_BLK))(order_keys)
    slot_ids = jnp.arange(MAXP, dtype=jnp.int32)
    layer_ids = slot_ids // TILES_BLK
    within = slot_ids % TILES_BLK
    local_rows = row_orders[:, within]
    shift_table = jnp.concatenate([jnp.zeros((SECTIONS * N_BLK, 1), jnp.int32), offsets.astype(jnp.int32)], axis=1)
    shifts = shift_table[:, layer_ids]
    block_of = (jnp.arange(SECTIONS * N_BLK, dtype=jnp.int32) % N_BLK)[:, None]
    col_tiles = (block_of * TILES_BLK + local_rows + shifts) % TILES_SEC
    tiles = jnp.stack([local_rows, col_tiles]).reshape(2, SECTIONS, N_BLK * MAXP)
    return (tiles.astype(jnp.int32), counts)


def draw_tile_pairs(key, part):
    return pair_plan(key)[0]


def draw_pair_counts(key, part):
    return pair_plan(key)[1]


def draw_column_pot(key, part):
    values = 0.5 * jnp.clip(jax.random.normal(jax.random.fold_in(key, 23), (SECTIONS, CELLS), jnp.float32), -6.0, 6.0)
    return values.astype(jnp.bfloat16)


def block_levels(own_key, dims, cuts, least, top_value):
    level = 1.0
    for position, blocks in cuts:
        heights = jax.random.uniform(jax.random.fold_in(jax.random.fold_in(own_key, 6), position), (blocks,), jnp.float32, least / len(cuts), top_value / len(cuts))
        level = level * jnp.repeat(jnp.exp(heights), dims[position] // blocks).reshape((-1,) + (1,) * (len(dims) - 1 - position))
    return level


def gaussian(rng, shape, width, bound, pieces=(), kind=jnp.bfloat16):
    gain = block_levels(rng, shape, pieces, -0.22, 0.18) if pieces else 1.0
    drawn = jax.random.normal(rng, shape, jnp.float32) * width * gain
    return jnp.minimum(jnp.maximum(drawn, -bound), bound).astype(kind)


def setup_inputs(seed: int = 0) -> dict:
    keys = jax.random.split(jax.random.key(seed), 6)
    features = gaussian(keys[0], (SECTIONS, FEAT, CELLS), 1.0, 6.0, ((0, 8), (2, 4)))
    programs = gaussian(keys[1], (SECTIONS, PROGS, CELLS), 1.0, 6.0, ((0, 8), (2, 4)))
    column_pot = draw_column_pot(jax.random.fold_in(keys[5], 71), 0)
    tile_pairs = draw_tile_pairs(jax.random.fold_in(keys[5], 71), 0)
    pair_counts = draw_pair_counts(jax.random.fold_in(keys[5], 71), 0)
    return {"features": features, "programs": programs, "column_pot": column_pot, "tile_pairs": tile_pairs, "pair_counts": pair_counts}


EPSILON = 0.05
NEG_FILL = -1.0e30


def merge_lse(first_lse, second_lse):
    highest = jnp.maximum(first_lse[0], second_lse[0])
    return (highest, first_lse[1] * jnp.exp(first_lse[0] - highest) + second_lse[1] * jnp.exp(second_lse[0] - highest))


def tile_cost(row_x, row_sq, col_x, col_sq, row_tile, col_tile):
    row_block = lax.dynamic_slice_in_dim(row_x, row_tile * TILE, TILE, 1)
    col_block = lax.dynamic_slice_in_dim(col_x, col_tile * TILE, TILE, 1)
    inner = lax.dot_general(row_block, col_block, (((0,), (0,)), ((), ())), preferred_element_type=jnp.float32)
    row_part = lax.dynamic_slice_in_dim(row_sq, row_tile * TILE, TILE, 0)
    col_part = lax.dynamic_slice_in_dim(col_sq, col_tile * TILE, TILE, 0)
    return (row_part[:, None] + col_part[None, :] - 2.0 * inner) / FEAT


def fold_lse(carry_lse, scores, offset, reduce_axis, usable):
    tile_max = jnp.max(scores, axis=reduce_axis)
    tile_sum = jnp.sum(jnp.exp(scores - jnp.expand_dims(tile_max, reduce_axis)), axis=reduce_axis)
    tile_max = jnp.where(usable, tile_max, NEG_FILL)
    tile_sum = jnp.where(usable, tile_sum, 0.0)
    old_max = lax.dynamic_slice_in_dim(carry_lse[0], offset, TILE, 0)
    old_sum = lax.dynamic_slice_in_dim(carry_lse[1], offset, TILE, 0)
    new_max, new_sum = merge_lse((old_max, old_sum), (tile_max, tile_sum))
    return (lax.dynamic_update_slice_in_dim(carry_lse[0], new_max, offset, 0), lax.dynamic_update_slice_in_dim(carry_lse[1], new_sum, offset, 0))


def one_plan(row_x, col_x, row_ext, col_ext, col_pot, row_tiles, col_tiles, usable):
    row_sq = jnp.sum(jnp.square(row_x.astype(jnp.float32)), axis=0)
    col_sq = jnp.sum(jnp.square(col_x.astype(jnp.float32)), axis=0)
    pot_in = col_pot.astype(jnp.float32)
    empty = (jnp.full((CELLS,), NEG_FILL, jnp.float32), jnp.zeros((CELLS,), jnp.float32))

    def row_pass(carry_lse, item):
        row_tile, col_tile, active = item
        cost = tile_cost(row_x, row_sq, col_x, col_sq, row_tile, col_tile)
        column = lax.dynamic_slice_in_dim(pot_in, col_tile * TILE, TILE, 0)
        scores = (column[None, :] - cost) / EPSILON
        return fold_lse(carry_lse, scores, row_tile * TILE, 1, active), 0

    row_lse = lax.scan(row_pass, empty, (row_tiles, col_tiles, usable))[0]
    row_pot = -EPSILON * (row_lse[0] + jnp.log(row_lse[1]))

    def col_pass(carry_lse, item):
        row_tile, col_tile, active = item
        cost = tile_cost(row_x, row_sq, col_x, col_sq, row_tile, col_tile)
        rows_here = lax.dynamic_slice_in_dim(row_pot, row_tile * TILE, TILE, 0)
        scores = (rows_here[:, None] - cost) / EPSILON
        return fold_lse(carry_lse, scores, col_tile * TILE, 0, active), 0

    col_lse = lax.scan(col_pass, empty, (row_tiles, col_tiles, usable))[0]
    col_new = -EPSILON * (col_lse[0] + jnp.log(col_lse[1]))
    zero_num = jnp.zeros((PROGS + 1, CELLS), jnp.float32)

    def plan_pass(sums, item):
        row_tile, col_tile, active = item
        row_num, col_num = sums
        cost = tile_cost(row_x, row_sq, col_x, col_sq, row_tile, col_tile)
        rows_here = lax.dynamic_slice_in_dim(row_pot, row_tile * TILE, TILE, 0)
        cols_here = lax.dynamic_slice_in_dim(col_new, col_tile * TILE, TILE, 0)
        plan = jnp.exp((rows_here[:, None] + cols_here[None, :] - cost) / EPSILON)
        plan = jnp.where(active, plan, 0.0).astype(jnp.bfloat16)
        col_prog = lax.dynamic_slice_in_dim(col_ext, col_tile * TILE, TILE, 1)
        row_prog = lax.dynamic_slice_in_dim(row_ext, row_tile * TILE, TILE, 1)
        to_rows = lax.dot_general(col_prog, plan, (((1,), (1,)), ((), ())), preferred_element_type=jnp.float32)
        to_cols = lax.dot_general(row_prog, plan, (((1,), (0,)), ((), ())), preferred_element_type=jnp.float32)
        old_rows = lax.dynamic_slice_in_dim(row_num, row_tile * TILE, TILE, 1)
        old_cols = lax.dynamic_slice_in_dim(col_num, col_tile * TILE, TILE, 1)
        row_num = lax.dynamic_update_slice_in_dim(row_num, old_rows + to_rows, row_tile * TILE, 1)
        col_num = lax.dynamic_update_slice_in_dim(col_num, old_cols + to_cols, col_tile * TILE, 1)
        return (row_num, col_num), 0

    row_num, col_num = lax.scan(plan_pass, (zero_num, zero_num), (row_tiles, col_tiles, usable))[0]
    return row_pot, col_new, row_num, col_num


def run_plan(packed):
    return one_plan(*packed)


def reference(features, programs, column_pot, tile_pairs, pair_counts):
    ones_row = jnp.ones((SECTIONS, 1, CELLS), jnp.bfloat16)
    extended = jnp.concatenate([programs, ones_row], axis=1)
    slot_ids = jnp.arange(SLOTS, dtype=jnp.int32)
    owners = slot_ids // MAXP
    row_tiles = (tile_pairs[0] + owners[None, :] * TILES_BLK).astype(jnp.int32)
    col_tiles = tile_pairs[1].astype(jnp.int32)
    usable = (slot_ids % MAXP)[None, :] < jnp.repeat(pair_counts, MAXP, axis=1)
    packed = (features[:-1], features[1:], extended[:-1], extended[1:], column_pot[:-1], row_tiles[:-1], col_tiles[:-1], usable[:-1])
    row_pot, col_pot, row_num, col_num = lax.map(run_plan, packed)
    zero_row = jnp.zeros((1, CELLS), jnp.float32)
    zero_num = jnp.zeros((1, PROGS + 1, CELLS), jnp.float32)
    row_potential = jnp.concatenate([row_pot, zero_row], axis=0)
    column_potential = jnp.concatenate([col_pot, zero_row], axis=0)
    totals = jnp.concatenate([row_num, zero_num], axis=0) + jnp.concatenate([zero_num, col_num], axis=0)
    smoothed = (totals[:, :PROGS] / totals[:, PROGS:]).astype(jnp.bfloat16)
    return smoothed, row_potential, column_potential
```

```python
import functools
import math

import jax
import jax.numpy as jnp
from jax import lax
from jax.experimental import pallas as pl
from jax.experimental.pallas import tpu as pltpu
from jax.sharding import PartitionSpec as P

TILE = 512
EPSILON = 0.05
LOG2E = math.log2(math.e)
NEG = -1e30
UNROLL = 2
SPLITS = 2
WIDTH = TILE // SPLITS
LANES = 128
MESH = pl.DeviceIdType.MESH


def depth_of(feat):
    return -(-(feat + 8) // 16) * 16


def ext_of(progs):
    return -(-(progs + 1) // 16) * 16


def gain_of(feat):
    return 2.0 * LOG2E / (feat * EPSILON)


def split3(value):
    hi = value.astype(jnp.bfloat16).astype(jnp.float32)
    rest = value - hi
    mid = rest.astype(jnp.bfloat16).astype(jnp.float32)
    return hi, mid, rest - mid


def rows_of(pieces, width):
    index = lax.broadcasted_iota(jnp.int32, (8, width), 0)
    block = jnp.zeros((8, width), jnp.float32)
    for place, piece in enumerate(pieces):
        block = jnp.where(index == place, piece, block)
    return block


def sum_squares(cells):
    return jnp.sum(cells * cells, axis=0, keepdims=True)


def lane_of(owner, place, blocks):
    kinds = blocks // SPLITS
    return (place * kinds + owner // SPLITS) * TILE + (owner % SPLITS) * WIDTH


def greet(targets):
    barrier = pltpu.get_barrier_semaphore()
    expected = jnp.int32(0)
    for used, sec, blk in targets:

        @pl.when(used)
        def _():
            pl.semaphore_signal(barrier, inc=1, device_id=(sec, blk), device_id_type=MESH)

        expected = expected + jnp.where(used, 1, 0)
    pl.semaphore_wait(barrier, expected)


def send(src, dst, sems, place, sec, blk):
    return pltpu.make_async_remote_copy(
        src_ref=src, dst_ref=dst, send_sem=sems[0].at[place], recv_sem=sems[1].at[place],
        device_id=(sec, blk), device_id_type=MESH,
    )


def mates_of(blk, blocks):
    core = blk + 1 - 2 * (blk % 2)
    across = (blk + 2) % blocks
    corner = core + 2 - 4 * (core // 2)
    return core, across, corner


def ext_tail(progs, width):
    index = lax.broadcasted_iota(jnp.int32, (ext_of(progs) - progs, width), 0)
    return jnp.where(index == 0, 1.0, 0.0).astype(jnp.bfloat16)


FEAT_CHUNKS = 4
PROG_CHUNKS = 2


def gather_kernel(counts, x_ref, prog_ref, pot_ref, pair_ref, count_ref,
                  xt_ref, y_ref, sq_ref, ext_next_ref, ext_own_ref, pairs_ref, counts_ref,
                  xs, progs_all, own_x, own_p, pots, build, send_sem, recv_sem, mate_send, mate_recv):
    n_sec, blocks = counts
    sec, blk = lax.axis_index("sec"), lax.axis_index("blk")
    feat, cells_blk = x_ref.shape
    progs = prog_ref.shape[0]
    depth = depth_of(feat)
    aux = depth - 8
    tiles_blk = cells_blk // TILE
    tiles = tiles_blk * blocks
    held_blk = tiles_blk * SPLITS // blocks
    has_to, has_from = sec > 0, sec < n_sec - 1
    core, across, corner = mates = mates_of(blk, blocks)
    greet(
        [(has_to, sec - 1, blk), (has_from, sec + 1, blk)] + [(sec >= 0, sec, mate) for mate in mates]
    )
    sems, mate_sems = (send_sem, recv_sem), (mate_send, mate_recv)
    feat_step, prog_step = cells_blk // FEAT_CHUNKS, cells_blk // PROG_CHUNKS
    chunks = [(x_ref, xs, n * feat_step, feat_step) for n in range(FEAT_CHUNKS)]
    chunks += [(prog_ref, progs_all, n * prog_step, prog_step) for n in range(PROG_CHUNKS)]

    def first(c):
        src, buffer, start, size = chunks[c]
        return send(
            src.at[:, start : start + size], buffer.at[blk, :, start : start + size], sems, 4 * c, sec - 1, blk
        )

    def share(c, kind):
        _, buffer, start, size = chunks[c]
        slot = buffer.at[across if kind == 2 else blk, :, start : start + size]
        return send(slot, slot, sems, 4 * c + 1 + kind, sec, across if kind == 0 else core)

    def to_mate(k):
        mate = mates[k]
        copies = [(pot_ref, pots.at[blk]), (pair_ref, pairs_ref.at[blk]), (count_ref, counts_ref.at[blk])]
        for place in range(held_blk):
            start = pl.multiple_of(lane_of(mate, place, blocks), WIDTH)
            copies.append((x_ref.at[:, pl.ds(start, WIDTH)], own_x.at[blk, place]))
        for place in range(held_blk):
            start = pl.multiple_of(lane_of(mate, place, blocks), WIDTH)
            copies.append((prog_ref.at[:, pl.ds(start, WIDTH)], own_p.at[blk, place]))
        per = len(copies)
        return [send(src, dst, mate_sems, per * k + n, sec, mate) for n, (src, dst) in enumerate(copies)]

    @pl.when(has_to)
    def _():
        for c in range(len(chunks)):
            first(c).start()

    to_mates = [to_mate(k) for k in range(3)]
    for n in range(len(to_mates[0])):
        for k in (1, 2, 0):
            to_mates[k][n].start()

    build[...] = jnp.zeros_like(build)
    build[aux : aux + 8, :] = rows_of([1.0] * 3, WIDTH)
    row = lax.broadcasted_iota(jnp.int32, (depth, TILE), 0)
    y_ref[tiles] = jnp.where(row == aux, NEG, 0.0).astype(jnp.bfloat16)
    ext_next_ref[tiles] = jnp.zeros(ext_next_ref.shape[1:], jnp.bfloat16)
    for place in range(held_blk):
        start = pl.multiple_of(lane_of(blk, place, blocks), WIDTH)
        own_x[blk, place] = x_ref[:, pl.ds(start, WIDTH)]
        own_p[blk, place] = prog_ref[:, pl.ds(start, WIDTH)]
    pots[blk] = pot_ref[...]
    pairs_ref[blk] = pair_ref[...]
    counts_ref[blk] = count_ref[...]

    def build_own(owner):
        for place in range(held_blk):
            held = owner * held_blk + place
            cells = own_x[owner, place].astype(jnp.float32)
            build[0:feat, :] = cells
            xt_ref[held] = build[...].T.astype(jnp.bfloat16)
            sq_ref[owner, place : place + 1, :] = sum_squares(cells)
            ext_own_ref[held, 0:progs, :] = own_p[owner, place]
            ext_own_ref[held, progs:, :] = ext_tail(progs, WIDTH)

    ones = jnp.ones((1, TILE), jnp.float32)

    def build_next(owner, c):
        source, _, begin, size = chunks[c]
        for start in range(begin, begin + size, TILE):
            tile = owner * tiles_blk + start // TILE
            if source is x_ref:
                raw = xs[owner, :, start : start + TILE]
                cells = raw.astype(jnp.float32)
                pot = pots[owner, :, start : start + TILE].astype(jnp.float32)
                bias = pot * (feat / 2) - sum_squares(cells) * 0.5
                y_ref[tile, 0:feat, :] = raw
                y_ref[tile, feat:aux, :] = jnp.zeros((aux - feat, TILE), jnp.bfloat16)
                y_ref[tile, aux:depth, :] = rows_of(split3(bias) + (ones,) * 3, TILE).astype(jnp.bfloat16)
            else:
                ext_next_ref[tile, 0:progs, :] = progs_all[owner, :, start : start + TILE]
                ext_next_ref[tile, progs:, :] = ext_tail(progs, TILE)

    build_own(blk)
    for k in range(3):
        for copy in to_mates[k][:3]:
            copy.wait_recv()

    @pl.when(has_from)
    def _():
        for turn in range(len(chunks) + 2):
            if turn < len(chunks):
                first(turn).wait_recv()
                share(turn, 0).start()
                share(turn, 1).start()
                build_next(blk, turn)
            if 0 <= turn - 1 < len(chunks):
                share(turn - 1, 0).wait_recv()
                share(turn - 1, 2).start()
                build_next(across, turn - 1)
                share(turn - 1, 1).wait_recv()
                build_next(core, turn - 1)
            if 0 <= turn - 2 < len(chunks):
                share(turn - 2, 2).wait_recv()
                build_next(corner, turn - 2)

    for k, mate in enumerate(mates):
        for copy in to_mates[k][3:]:
            copy.wait_recv()
        build_own(mate)

    @pl.when(has_to)
    def _():
        for c in range(len(chunks)):
            first(c).wait_send()

    @pl.when(has_from)
    def _():
        for c in range(len(chunks)):
            for kind in range(3):
                share(c, kind).wait_send()

    for k in range(3):
        for copy in to_mates[k]:
            copy.wait_send()


def listed_pairs(pairs_ref, counts_ref, mine, other, blocks, tiles_blk, tiles):
    kinds = blocks // SPLITS
    kind = lax.axis_index("blk") // SPLITS

    def of_block(block, place):
        def one(slot, at):
            row = pairs_ref[block, 0, 0, slot] + block * tiles_blk
            mine[at] = row // kinds
            other[at] = pairs_ref[block, 1, 0, slot]
            return at + jnp.where(row % kinds == kind, 1, 0)

        return lax.fori_loop(0, counts_ref[block, 0, 0], one, place)

    total = lax.fori_loop(0, blocks, of_block, 0)
    last = jnp.where(total > 0, mine[jnp.maximum(total - 1, 0)], 0)
    for extra in range(2 * UNROLL):
        mine[total + extra] = last
        other[total + extra] = tiles
    return (total + UNROLL - 1) // UNROLL


def over_pairs(groups, ready, xt, y_ref, mine, other, use):
    def make(at, place):
        ready[place][...] = jnp.dot(xt[mine[at]], y_ref[other[at]], preferred_element_type=jnp.float32)

    make(0, 0)

    def group(index, carry):
        for step in range(UNROLL):
            at = index * UNROLL + step
            make(at + 1, (step + 1) % UNROLL)
            use(ready[step], mine[at], other[at])
        return carry

    lax.fori_loop(0, groups, group, 0)


STRIP = 64


def stats_kernel(dims, pairs_ref, counts_ref, xt_ref, y_ref, sq_ref, rp_ref, xt_out, cl_ref,
                 top_row, sum_row, top_col, sum_col, mine, other, *ready):
    feat, blocks, tiles_blk = dims
    tiles = blocks * tiles_blk
    held_blk = tiles_blk * SPLITS // blocks
    held = blocks * held_blk
    gain = gain_of(feat)
    aux = depth_of(feat) - 8
    at_end = lax.axis_index("sec") == lax.axis_size("sec") - 1
    groups = listed_pairs(pairs_ref, counts_ref, mine, other, blocks, tiles_blk, tiles)
    for ref in (top_row, top_col):
        ref[...] = jnp.full_like(ref, NEG)
    for ref in (sum_row, sum_col):
        ref[...] = jnp.zeros_like(ref)
    parts = TILE // LANES

    def row_use(scores, row, col):
        for start in range(0, WIDTH, STRIP):
            here = pl.ds(start, STRIP)
            pieces = [scores[here, n * LANES : (n + 1) * LANES] for n in range(parts)]
            old = top_row[row, here, :]
            new = functools.reduce(jnp.maximum, pieces, old)
            part = sum_row[row, here, :] * jnp.exp2((old - new) * gain)
            for piece in pieces:
                part = part + jnp.exp2((piece - new) * gain)
            sum_row[row, here, :] = part
            top_row[row, here, :] = new

    over_pairs(groups, ready, xt_ref, y_ref, mine, other, row_use)
    lane = lax.broadcasted_iota(jnp.int32, (WIDTH, LANES), 1)
    record_lane = lax.broadcasted_iota(jnp.int32, (WIDTH, xt_ref.shape[2]), 1)
    columns = jnp.zeros((WIDTH, LANES), jnp.float32)
    for row in range(held):
        tops = top_row[row]
        top = jnp.max(tops, axis=1, keepdims=True)
        total = jnp.sum(sum_row[row] * jnp.exp2((tops - top) * gain), axis=1, keepdims=True)
        level = top + jnp.log2(total) * (1.0 / gain)
        columns = jnp.where(lane == row, level, columns)
        record = xt_ref[row].astype(jnp.float32)
        for place, piece in enumerate(split3(-level)):
            record = jnp.where(record_lane == aux + 3 + place, piece, record)
        xt_out[row] = record.astype(jnp.bfloat16)
    levels = columns.T
    for row in range(held):
        owner, place = row // held_blk, row % held_blk
        potential = (sq_ref[owner, place : place + 1, :] - 2.0 * levels[row : row + 1, :]) * (1.0 / feat)
        rp_ref[owner, place : place + 1, :] = jnp.where(at_end, 0.0, potential)

    def col_use(scores, row, col):
        for n in range(parts):
            here = slice(n * LANES, (n + 1) * LANES)
            block = scores[:, here].reshape(WIDTH // 8, 8, LANES)
            old = top_col[col, :, here]
            new = jnp.maximum(old, jnp.max(block, axis=0))
            part = jnp.sum(jnp.exp2((block - new) * gain), axis=0)
            sum_col[col, :, here] = sum_col[col, :, here] * jnp.exp2((old - new) * gain) + part
            top_col[col, :, here] = new

    over_pairs(groups, ready, xt_out, y_ref, mine, other, col_use)
    for col in range(tiles):
        tops = top_col[col]
        top = jnp.max(tops, axis=0, keepdims=True)
        total = jnp.sum(sum_col[col] * jnp.exp2((tops - top) * gain), axis=0, keepdims=True)
        level = jnp.where(total > 0.0, top + jnp.log2(total) * (1.0 / gain), NEG)
        cl_ref[col : col + 1, :] = level


def merge_kernel(counts, feat, rp_ref, cl_ref, level_ref, home_ref, parts, send_sem, recv_sem):
    n_sec, blocks = counts
    sec, blk = lax.axis_index("sec"), lax.axis_index("blk")
    tiles = cl_ref.shape[0]
    gain = gain_of(feat)
    mates = mates_of(blk, blocks)
    sems = (send_sem, recv_sem)
    greet([(sec >= 0, sec, mate) for mate in mates])
    copies = []
    for k, mate in enumerate(mates):
        copies.append(send(cl_ref, parts.at[blk], sems, 2 * k, sec, mate))
        copies.append(send(rp_ref.at[mate], home_ref.at[blk], sems, 2 * k + 1, sec, mate))
    for k in (1, 2, 0):
        for copy in copies[2 * k : 2 * k + 2]:
            copy.start()
    parts[blk] = cl_ref[...]
    home_ref[blk] = rp_ref[blk]
    level_ref[tiles:, :] = jnp.zeros((level_ref.shape[0] - tiles, TILE), jnp.float32)
    for copy in copies:
        copy.wait_recv()
    levels = [parts[n] for n in range(blocks)]
    top = functools.reduce(jnp.maximum, levels)
    total = functools.reduce(jnp.add, [jnp.exp2((level - top) * gain) for level in levels])
    level_ref[0:tiles, :] = top + jnp.log2(total) * (1.0 / gain)
    for copy in copies:
        copy.wait_send()


def plan_kernel(dims, pairs_ref, counts_ref, xt_ref, y_ref, level_ref, ext_next_ref, ext_own_ref, pot_ref, home_ref,
                fnum_ref, fden_ref, bnum_ref, bden_ref, rows_ref, cols_ref, acc_row, acc_col, mine, other, *ready):
    feat, blocks, tiles_blk = dims
    tiles = blocks * tiles_blk
    held_blk = tiles_blk * SPLITS // blocks
    held = blocks * held_blk
    gain = gain_of(feat)
    progs = fnum_ref.shape[1]
    at_end = lax.axis_index("sec") == lax.axis_size("sec") - 1
    groups = listed_pairs(pairs_ref, counts_ref, mine, other, blocks, tiles_blk, tiles)
    acc_row[...] = jnp.zeros_like(acc_row)
    acc_col[...] = jnp.zeros_like(acc_col)
    for owner in range(blocks):
        for place in range(held_blk):
            start = lane_of(owner, place, blocks)
            rows_ref[:, start : start + WIDTH] = home_ref[owner, place : place + 1, :]
    blk = lax.axis_index("blk")
    for tile in range(tiles_blk):
        here = slice(tile * TILE, (tile + 1) * TILE)
        level = level_ref[pl.ds(blk * tiles_blk + tile, 1), :]
        potential = pot_ref[:, here].astype(jnp.float32) - level * (2.0 / feat)
        cols_ref[:, here] = jnp.where(at_end, 0.0, potential)

    def use(scores, row, col):
        level = level_ref[pl.ds(col, 1), :]
        plan = jnp.exp2((scores[...] - level) * gain).astype(jnp.bfloat16)
        acc_row[row] += lax.dot_general(
            ext_next_ref[col], plan, (((1,), (1,)), ((), ())), preferred_element_type=jnp.float32
        )
        acc_col[col] += jnp.dot(ext_own_ref[row], plan, preferred_element_type=jnp.float32)

    over_pairs(groups, ready, xt_ref, y_ref, mine, other, use)
    for row in range(held):
        owner, place = row // held_blk, row % held_blk
        fnum_ref[owner, :, place * WIDTH : (place + 1) * WIDTH] = acc_row[row, 0:progs, :].astype(jnp.bfloat16)
        fden_ref[owner, place : place + 1, :] = acc_row[row, progs : progs + 1, :]
    for col in range(tiles):
        owner, place = col // tiles_blk, col % tiles_blk
        bnum_ref[owner, place] = acc_col[col, 0:progs, :].astype(jnp.bfloat16)
        bden_ref[owner, place : place + 1, :] = acc_col[col, progs : progs + 1, :]


def finish_kernel(counts, fnum_ref, fden_ref, bnum_ref, bden_ref, out_ref,
                  hn, hd, an, ad, keep, keep_den, go, go_den, bn, bd, ship, ship_den, cn, cd,
                  send_sem, recv_sem):
    n_sec, blocks = counts
    sec, blk = lax.axis_index("sec"), lax.axis_index("blk")
    tiles_blk = bnum_ref.shape[1]
    held_blk = fden_ref.shape[1]
    kinds = blocks // SPLITS
    has_to, has_from = sec < n_sec - 1, sec > 0
    core, across, corner = mates = mates_of(blk, blocks)
    me, side = blk % 2, blk // 2
    sems = (send_sem, recv_sem)
    greet(
        [(has_to, sec + 1, blk), (has_from, sec - 1, blk)] + [(sec >= 0, sec, mate) for mate in mates]
    )

    def homeward(k, n):
        mate = mates[k]
        src, dst = ((fnum_ref, hn), (fden_ref, hd))[n]
        return send(src.at[mate], dst.at[blk], sems, 2 * k + n, sec, mate)

    steps = tiles_blk + 1
    base = 6

    def pair(t, far):
        place = 1 - side if far else side
        source = 2 * place + 1 - me
        number = base + 2 * t + (0 if far else 1)
        slot = 0 if far else 1
        if t == tiles_blk:
            return send(bden_ref.at[source], ad.at[slot], sems, number, sec, core)
        return send(bnum_ref.at[source, t], an.at[slot, t], sems, number, sec, core)

    def cross(t):
        number = base + 2 * steps + t
        if t == tiles_blk:
            return send(go_den, bd, sems, number, sec, across)
        return send(go.at[t], bn.at[t], sems, number, sec, across)

    def onward(t):
        number = base + 3 * steps + t
        if t == tiles_blk:
            return send(ship_den, cd, sems, number, sec + 1, blk)
        return send(ship.at[t], cn.at[t], sems, number, sec + 1, blk)

    order = [tiles_blk] + list(range(tiles_blk))

    @pl.when(has_to)
    def _():
        for t in order:
            pair(t, True).start()
        for t in order:
            pair(t, False).start()

    for k in (1, 2, 0):
        for n in range(2):
            homeward(k, n).start()
    hn[blk] = fnum_ref[blk]
    hd[blk] = fden_ref[blk]

    @pl.when(has_to)
    def _():
        far, near = 2 * (1 - side) + me, 2 * side + me
        for t in order:
            pair(t, True).wait_recv()
            if t == tiles_blk:
                go_den[...] = bden_ref[far] + ad[0]
            else:
                go[t] = (bnum_ref[far, t].astype(jnp.float32) + an[0, t].astype(jnp.float32)).astype(jnp.bfloat16)
            cross(t).start()
        for t in order:
            pair(t, False).wait_recv()
            if t == tiles_blk:
                keep_den[...] = bden_ref[near] + ad[1]
            else:
                keep[t] = bnum_ref[near, t].astype(jnp.float32) + an[1, t].astype(jnp.float32)
        for t in order:
            cross(t).wait_recv()
            if t == tiles_blk:
                ship_den[...] = keep_den[...] + bd[...]
            else:
                ship[t] = (keep[t] + bn[t].astype(jnp.float32)).astype(jnp.bfloat16)
            onward(t).start()

    for k in range(3):
        for n in range(2):
            homeward(k, n).wait_recv()

    @pl.when(jnp.logical_not(has_from))
    def _():
        cn[...] = jnp.zeros_like(cn)
        cd[...] = jnp.zeros_like(cd)

    for t in order:

        @pl.when(has_from)
        def _():
            onward(t).wait_recv()

        if t == tiles_blk:
            continue
        place, kind = t // kinds, t % kinds
        owners = [kind * SPLITS + n for n in range(SPLITS)]
        here = slice(place * WIDTH, (place + 1) * WIDTH)
        for n, owner in enumerate(owners):
            part = slice(n * WIDTH, (n + 1) * WIDTH)
            number = hn[owner, :, here].astype(jnp.float32) + cn[t, :, part].astype(jnp.float32)
            weight = hd[owner, place : place + 1, :] + cd[t : t + 1, part]
            start = t * TILE + n * WIDTH
            out_ref[:, start : start + WIDTH] = (number / weight).astype(jnp.bfloat16)

    for k in range(3):
        for n in range(2):
            homeward(k, n).wait_send()

    @pl.when(has_to)
    def _():
        for t in range(steps):
            pair(t, True).wait_send()
            pair(t, False).wait_send()
            cross(t).wait_send()
            onward(t).wait_send()


def in_vmem(count):
    return [pl.BlockSpec(memory_space=pltpu.VMEM)] * count


def exchange(kernel, number, out_shape, operands, scratch):
    outs = jax.tree.map(lambda _: pl.BlockSpec(memory_space=pltpu.VMEM), out_shape)
    return pl.pallas_call(
        kernel, out_shape=out_shape, in_specs=in_vmem(len(operands)), out_specs=outs, scratch_shapes=scratch,
        compiler_params=pltpu.CompilerParams(collective_id=number, has_side_effects=True),
    )(*operands)


def call(kernel, out_shape, operands, scratch):
    outs = jax.tree.map(lambda _: pl.BlockSpec(memory_space=pltpu.VMEM), out_shape)
    return pl.pallas_call(
        kernel, out_shape=out_shape,
        in_specs=[pl.BlockSpec(memory_space=pltpu.SMEM)] * 2 + in_vmem(len(operands) - 2),
        out_specs=outs, scratch_shapes=scratch,
    )(*operands)


def body(features, programs, column_pot, tile_pairs, pair_counts):
    feat, cells_blk = features.shape[1:]
    progs = programs.shape[1]
    tiles_blk = cells_blk // TILE
    most = tile_pairs.shape[2]
    blocks, n_sec = lax.axis_size("blk"), lax.axis_size("sec")
    tiles = tiles_blk * blocks
    held_blk = tiles_blk * SPLITS // blocks
    held = blocks * held_blk
    dims = (feat, blocks, tiles_blk)
    counts = (n_sec, blocks)
    depth, ext = depth_of(feat), ext_of(progs)
    f32, bf16, i32 = jnp.float32, jnp.bfloat16, jnp.int32
    shape, vmem = jax.ShapeDtypeStruct, pltpu.VMEM

    def dma(number):
        return [pltpu.SemaphoreType.DMA((number,))] * 2

    mate_copies = (blocks - 1) * (2 * held_blk + 3)
    xt, y, sq, ext_next, ext_own, pairs, all_counts = exchange(
        functools.partial(gather_kernel, counts), 0,
        (
            shape((held, WIDTH, depth), bf16),
            shape((tiles + 1, depth, TILE), bf16),
            shape((blocks, held_blk, WIDTH), f32),
            shape((tiles + 1, ext, TILE), bf16),
            shape((held, ext, WIDTH), bf16),
            shape((blocks, 2, 1, most), i32),
            shape((blocks, 1, 1), i32),
        ),
        (features[0], programs[0], column_pot, tile_pairs, pair_counts),
        [
            vmem((blocks, feat, cells_blk), bf16),
            vmem((blocks, progs, cells_blk), bf16),
            vmem((blocks, held_blk, feat, WIDTH), bf16),
            vmem((blocks, held_blk, progs, WIDTH), bf16),
            vmem((blocks, 1, cells_blk), bf16),
            vmem((depth, WIDTH), f32),
            *dma(4 * (FEAT_CHUNKS + PROG_CHUNKS)), *dma(mate_copies),
        ],
    )
    index = pltpu.SMEM((blocks * most + 2 * UNROLL,), i32)
    ready = [vmem((WIDTH, TILE), f32)] * UNROLL
    pots = shape((blocks, held_blk, WIDTH), f32)
    rp, xt2, cl = call(
        functools.partial(stats_kernel, dims),
        (pots, shape((held, WIDTH, depth), bf16), shape((tiles, TILE), f32)),
        (pairs, all_counts, xt, y, sq),
        [
            vmem((held, WIDTH, LANES), f32), vmem((held, WIDTH, LANES), f32),
            vmem((tiles + 1, 8, TILE), f32), vmem((tiles + 1, 8, TILE), f32), index, index, *ready,
        ],
    )
    level, home = exchange(
        functools.partial(merge_kernel, counts, feat), 1, (shape((tiles + 8, TILE), f32), pots), (rp, cl),
        [vmem((blocks, tiles, TILE), f32), *dma(2 * (blocks - 1))],
    )
    line = shape((1, cells_blk), f32)
    fnum, fden, bnum, bden, row_out, col_out = call(
        functools.partial(plan_kernel, dims),
        (
            shape((blocks, progs, held_blk * WIDTH), bf16), pots,
            shape((blocks, tiles_blk, progs, TILE), bf16), shape((blocks, tiles_blk, TILE), f32), line, line,
        ),
        (pairs, all_counts, xt2, y, level, ext_next, ext_own, column_pot, home),
        [vmem((held, ext, WIDTH), f32), vmem((tiles + 1, ext, TILE), f32), index, index, *ready],
    )
    num, den = vmem((tiles_blk, progs, TILE), bf16), vmem((tiles_blk, TILE), f32)
    smoothed = exchange(
        functools.partial(finish_kernel, counts), 2, shape((progs, cells_blk), bf16), (fnum, fden, bnum, bden),
        [
            vmem((blocks, progs, held_blk * WIDTH), bf16), vmem((blocks, held_blk, WIDTH), f32),
            vmem((2, tiles_blk, progs, TILE), bf16), vmem((2, tiles_blk, TILE), f32),
            vmem((tiles_blk, progs, TILE), f32), den, num, den, num, den, num, den, num, den,
            *dma(6 + 4 * (tiles_blk + 1)),
        ],
    )
    return smoothed[None], row_out, col_out


def solution(mesh):
    in_specs = (
        P("sec", None, "blk"),
        P("sec", None, "blk"),
        P("sec", "blk"),
        P(None, "sec", "blk"),
        P("sec", "blk"),
    )
    out_specs = (P("sec", None, "blk"), P("sec", "blk"), P("sec", "blk"))
    return jax.shard_map(body, mesh=mesh, in_specs=in_specs, out_specs=out_specs, check_vma=False)
```

```python
import functools
import math

import jax
import jax.numpy as jnp
from jax import lax
from jax.experimental import pallas as pl
from jax.experimental.pallas import tpu as pltpu
from jax.sharding import PartitionSpec as P

TILE = 512
EPSILON = 0.05
LOG2E = math.log2(math.e)
NEG = -1e30
UNROLL = 2
SPLITS = 2
WIDTH = TILE // SPLITS
LANES = 128
VMEM_LIMIT = 24 << 20
MESH = pl.DeviceIdType.MESH


def depth_of(feat):
    return -(-(feat + 8) // 16) * 16


def ext_of(progs):
    return -(-(progs + 1) // 16) * 16


def gain_of(feat):
    return 2.0 * LOG2E / (feat * EPSILON)


def split3(value):
    hi = value.astype(jnp.bfloat16).astype(jnp.float32)
    rest = value - hi
    mid = rest.astype(jnp.bfloat16).astype(jnp.float32)
    return hi, mid, rest - mid


def rows_of(pieces, width):
    index = lax.broadcasted_iota(jnp.int32, (8, width), 0)
    block = jnp.zeros((8, width), jnp.float32)
    for place, piece in enumerate(pieces):
        block = jnp.where(index == place, piece, block)
    return block


def sum_squares(cells):
    return jnp.sum(cells * cells, axis=0, keepdims=True)


def lane_of(owner, place, blocks):
    kinds = blocks // SPLITS
    return (place * kinds + owner // SPLITS) * TILE + (owner % SPLITS) * WIDTH


def greet(targets):
    barrier = pltpu.get_barrier_semaphore()
    expected = jnp.int32(0)
    for used, sec, blk in targets:

        @pl.when(used)
        def _():
            pl.semaphore_signal(barrier, inc=1, device_id=(sec, blk), device_id_type=MESH)

        expected = expected + jnp.where(used, 1, 0)
    pl.semaphore_wait(barrier, expected)


def send(src, dst, sems, place, sec, blk):
    return pltpu.make_async_remote_copy(
        src_ref=src, dst_ref=dst, send_sem=sems[0].at[place], recv_sem=sems[1].at[place],
        device_id=(sec, blk), device_id_type=MESH,
    )


def mates_of(blk, blocks):
    core = blk + 1 - 2 * (blk % 2)
    across = (blk + 2) % blocks
    corner = core + 2 - 4 * (core // 2)
    return core, across, corner


def ext_tail(progs, width):
    index = lax.broadcasted_iota(jnp.int32, (ext_of(progs) - progs, width), 0)
    return jnp.where(index == 0, 1.0, 0.0).astype(jnp.bfloat16)


FEAT_CHUNKS = 4
PROG_CHUNKS = 2


def gather_kernel(counts, x_ref, prog_ref, pot_ref, pair_ref, count_ref,
                  xt_ref, y_ref, sq_ref, ext_next_ref, ext_own_ref, pairs_ref, counts_ref,
                  xs, progs_all, own_x, own_p, pots, build, send_sem, recv_sem, mate_send, mate_recv, local_sem):
    n_sec, blocks = counts
    sec, blk = lax.axis_index("sec"), lax.axis_index("blk")
    feat, cells_blk = x_ref.shape
    progs = prog_ref.shape[0]
    depth = depth_of(feat)
    aux = depth - 8
    tiles_blk = cells_blk // TILE
    tiles = tiles_blk * blocks
    held_blk = tiles_blk * SPLITS // blocks
    has_to, has_from = sec > 0, sec < n_sec - 1
    core, across, corner = mates = mates_of(blk, blocks)
    moves = [(pot_ref, pots.at[blk]), (pair_ref, pairs_ref.at[blk]), (count_ref, counts_ref.at[blk])]
    for place in range(held_blk):
        start = pl.multiple_of(lane_of(blk, place, blocks), WIDTH)
        moves.append((x_ref.at[:, pl.ds(start, WIDTH)], own_x.at[blk, place]))
        moves.append((prog_ref.at[:, pl.ds(start, WIDTH)], own_p.at[blk, place]))
    locals_ = [pltpu.make_async_copy(src, dst, local_sem.at[n]) for n, (src, dst) in enumerate(moves)]
    for copy in locals_:
        copy.start()
    greet(
        [(has_to, sec - 1, blk), (has_from, sec + 1, blk)] + [(sec >= 0, sec, mate) for mate in mates]
    )
    sems, mate_sems = (send_sem, recv_sem), (mate_send, mate_recv)
    feat_step, prog_step = cells_blk // FEAT_CHUNKS, cells_blk // PROG_CHUNKS
    chunks = [(x_ref, xs, n * feat_step, feat_step) for n in range(FEAT_CHUNKS)]
    chunks += [(prog_ref, progs_all, n * prog_step, prog_step) for n in range(PROG_CHUNKS)]

    def first(c):
        src, buffer, start, size = chunks[c]
        return send(
            src.at[:, start : start + size], buffer.at[blk, :, start : start + size], sems, 4 * c, sec - 1, blk
        )

    def share(c, kind):
        _, buffer, start, size = chunks[c]
        slot = buffer.at[across if kind == 2 else blk, :, start : start + size]
        return send(slot, slot, sems, 4 * c + 1 + kind, sec, across if kind == 0 else core)

    def to_mate(k):
        mate = mates[k]
        copies = [(pot_ref, pots.at[blk]), (pair_ref, pairs_ref.at[blk]), (count_ref, counts_ref.at[blk])]
        for place in range(held_blk):
            start = pl.multiple_of(lane_of(mate, place, blocks), WIDTH)
            copies.append((x_ref.at[:, pl.ds(start, WIDTH)], own_x.at[blk, place]))
        for place in range(held_blk):
            start = pl.multiple_of(lane_of(mate, place, blocks), WIDTH)
            copies.append((prog_ref.at[:, pl.ds(start, WIDTH)], own_p.at[blk, place]))
        per = len(copies)
        return [send(src, dst, mate_sems, per * k + n, sec, mate) for n, (src, dst) in enumerate(copies)]

    @pl.when(has_to)
    def _():
        for c in range(len(chunks)):
            first(c).start()

    to_mates = [to_mate(k) for k in range(3)]
    for n in range(len(to_mates[0])):
        for k in (1, 2, 0):
            to_mates[k][n].start()

    build[...] = jnp.zeros_like(build)
    build[aux : aux + 8, :] = rows_of([1.0] * 3, WIDTH)
    row = lax.broadcasted_iota(jnp.int32, (depth, TILE), 0)
    y_ref[tiles] = jnp.where(row == aux, NEG, 0.0).astype(jnp.bfloat16)
    ext_next_ref[tiles] = jnp.zeros(ext_next_ref.shape[1:], jnp.bfloat16)
    for copy in locals_:
        copy.wait()

    def build_own(owner):
        for place in range(held_blk):
            held = owner * held_blk + place
            cells = own_x[owner, place].astype(jnp.float32)
            build[0:feat, :] = cells
            xt_ref[held] = build[...].T.astype(jnp.bfloat16)
            sq_ref[owner, place : place + 1, :] = sum_squares(cells)
            ext_own_ref[held, 0:progs, :] = own_p[owner, place]
            ext_own_ref[held, progs:, :] = ext_tail(progs, WIDTH)

    ones = jnp.ones((1, TILE), jnp.float32)

    def build_next(owner, c):
        source, _, begin, size = chunks[c]
        for start in range(begin, begin + size, TILE):
            tile = owner * tiles_blk + start // TILE
            if source is x_ref:
                raw = xs[owner, :, start : start + TILE]
                cells = raw.astype(jnp.float32)
                pot = pots[owner, :, start : start + TILE].astype(jnp.float32)
                bias = pot * (feat / 2) - sum_squares(cells) * 0.5
                y_ref[tile, 0:feat, :] = raw
                y_ref[tile, feat:aux, :] = jnp.zeros((aux - feat, TILE), jnp.bfloat16)
                y_ref[tile, aux:depth, :] = rows_of(split3(bias) + (ones,) * 3, TILE).astype(jnp.bfloat16)
            else:
                ext_next_ref[tile, 0:progs, :] = progs_all[owner, :, start : start + TILE]
                ext_next_ref[tile, progs:, :] = ext_tail(progs, TILE)

    build_own(blk)
    for k in range(3):
        for copy in to_mates[k][:3]:
            copy.wait_recv()

    @pl.when(has_from)
    def _():
        for turn in range(len(chunks) + 2):
            if turn < len(chunks):
                first(turn).wait_recv()
                share(turn, 0).start()
                share(turn, 1).start()
                build_next(blk, turn)
            if 0 <= turn - 1 < len(chunks):
                share(turn - 1, 0).wait_recv()
                share(turn - 1, 2).start()
                build_next(across, turn - 1)
                share(turn - 1, 1).wait_recv()
                build_next(core, turn - 1)
            if 0 <= turn - 2 < len(chunks):
                share(turn - 2, 2).wait_recv()
                build_next(corner, turn - 2)

    for k, mate in enumerate(mates):
        for copy in to_mates[k][3:]:
            copy.wait_recv()
        build_own(mate)

    @pl.when(has_to)
    def _():
        for c in range(len(chunks)):
            first(c).wait_send()

    @pl.when(has_from)
    def _():
        for c in range(len(chunks)):
            for kind in range(3):
                share(c, kind).wait_send()

    for k in range(3):
        for copy in to_mates[k]:
            copy.wait_send()


def listed_pairs(pairs_ref, counts_ref, mine, other, blocks, tiles_blk, tiles):
    kinds = blocks // SPLITS
    kind = lax.axis_index("blk") // SPLITS

    def of_block(block, place):
        def one(slot, at):
            row = pairs_ref[block, 0, 0, slot] + block * tiles_blk
            mine[at] = row // kinds
            other[at] = pairs_ref[block, 1, 0, slot]
            return at + jnp.where(row % kinds == kind, 1, 0)

        return lax.fori_loop(0, counts_ref[block, 0, 0], one, place)

    total = lax.fori_loop(0, blocks, of_block, 0)
    last = jnp.where(total > 0, mine[jnp.maximum(total - 1, 0)], 0)
    for extra in range(2 * UNROLL):
        mine[total + extra] = last
        other[total + extra] = tiles
    return (total + UNROLL - 1) // UNROLL


def over_pairs(groups, ready, xt, y_ref, mine, other, use):
    def make(at, place):
        ready[place][...] = jnp.dot(xt[mine[at]], y_ref[other[at]], preferred_element_type=jnp.float32)

    make(0, 0)

    def group(index, carry):
        for step in range(UNROLL):
            at = index * UNROLL + step
            make(at + 1, (step + 1) % UNROLL)
            use(ready[step], mine[at], other[at])
        return carry

    lax.fori_loop(0, groups, group, 0)


STRIP = 64


def stats_kernel(dims, pairs_ref, counts_ref, xt_ref, y_ref, sq_ref, rp_ref, xt_out, cl_ref,
                 top_row, sum_row, top_col, sum_col, mine, other, *ready):
    feat, blocks, tiles_blk = dims
    tiles = blocks * tiles_blk
    held_blk = tiles_blk * SPLITS // blocks
    held = blocks * held_blk
    gain = gain_of(feat)
    aux = depth_of(feat) - 8
    at_end = lax.axis_index("sec") == lax.axis_size("sec") - 1
    groups = listed_pairs(pairs_ref, counts_ref, mine, other, blocks, tiles_blk, tiles)
    for ref in (top_row, top_col):
        ref[...] = jnp.full_like(ref, NEG)
    for ref in (sum_row, sum_col):
        ref[...] = jnp.zeros_like(ref)
    parts = TILE // LANES

    def row_use(scores, row, col):
        for start in range(0, WIDTH, STRIP):
            here = pl.ds(start, STRIP)
            pieces = [scores[here, n * LANES : (n + 1) * LANES] for n in range(parts)]
            old = top_row[row, here, :]
            new = functools.reduce(jnp.maximum, pieces, old)
            part = sum_row[row, here, :] * jnp.exp2((old - new) * gain)
            for piece in pieces:
                part = part + jnp.exp2((piece - new) * gain)
            sum_row[row, here, :] = part
            top_row[row, here, :] = new

    over_pairs(groups, ready, xt_ref, y_ref, mine, other, row_use)
    lane = lax.broadcasted_iota(jnp.int32, (WIDTH, LANES), 1)
    record_lane = lax.broadcasted_iota(jnp.int32, (WIDTH, xt_ref.shape[2]), 1)
    columns = jnp.zeros((WIDTH, LANES), jnp.float32)
    for row in range(held):
        tops = top_row[row]
        top = jnp.max(tops, axis=1, keepdims=True)
        total = jnp.sum(sum_row[row] * jnp.exp2((tops - top) * gain), axis=1, keepdims=True)
        level = top + jnp.log2(total) * (1.0 / gain)
        columns = jnp.where(lane == row, level, columns)
        record = xt_ref[row].astype(jnp.float32)
        for place, piece in enumerate(split3(-level)):
            record = jnp.where(record_lane == aux + 3 + place, piece, record)
        xt_out[row] = record.astype(jnp.bfloat16)
    levels = columns.T
    for row in range(held):
        owner, place = row // held_blk, row % held_blk
        potential = (sq_ref[owner, place : place + 1, :] - 2.0 * levels[row : row + 1, :]) * (1.0 / feat)
        rp_ref[owner, place : place + 1, :] = jnp.where(at_end, 0.0, potential)

    def col_use(scores, row, col):
        for n in range(parts):
            here = slice(n * LANES, (n + 1) * LANES)
            block = scores[:, here].reshape(WIDTH // 8, 8, LANES)
            old = top_col[col, :, here]
            new = jnp.maximum(old, jnp.max(block, axis=0))
            part = jnp.sum(jnp.exp2((block - new) * gain), axis=0)
            sum_col[col, :, here] = sum_col[col, :, here] * jnp.exp2((old - new) * gain) + part
            top_col[col, :, here] = new

    over_pairs(groups, ready, xt_out, y_ref, mine, other, col_use)
    for col in range(tiles):
        tops = top_col[col]
        top = jnp.max(tops, axis=0, keepdims=True)
        total = jnp.sum(sum_col[col] * jnp.exp2((tops - top) * gain), axis=0, keepdims=True)
        level = jnp.where(total > 0.0, top + jnp.log2(total) * (1.0 / gain), NEG)
        cl_ref[col : col + 1, :] = level


def merge_kernel(counts, feat, rp_ref, cl_ref, level_ref, home_ref, parts, send_sem, recv_sem):
    n_sec, blocks = counts
    sec, blk = lax.axis_index("sec"), lax.axis_index("blk")
    tiles = cl_ref.shape[0]
    gain = gain_of(feat)
    mates = mates_of(blk, blocks)
    sems = (send_sem, recv_sem)
    greet([(sec >= 0, sec, mate) for mate in mates])
    copies = []
    for k, mate in enumerate(mates):
        copies.append(send(cl_ref, parts.at[blk], sems, 2 * k, sec, mate))
        copies.append(send(rp_ref.at[mate], home_ref.at[blk], sems, 2 * k + 1, sec, mate))
    for k in (1, 2, 0):
        for copy in copies[2 * k : 2 * k + 2]:
            copy.start()
    parts[blk] = cl_ref[...]
    home_ref[blk] = rp_ref[blk]
    level_ref[tiles:, :] = jnp.zeros((level_ref.shape[0] - tiles, TILE), jnp.float32)
    for copy in copies:
        copy.wait_recv()
    levels = [parts[n] for n in range(blocks)]
    top = functools.reduce(jnp.maximum, levels)
    total = functools.reduce(jnp.add, [jnp.exp2((level - top) * gain) for level in levels])
    level_ref[0:tiles, :] = top + jnp.log2(total) * (1.0 / gain)
    for copy in copies:
        copy.wait_send()


def plan_kernel(dims, pairs_ref, counts_ref, xt_ref, y_ref, level_ref, ext_next_ref, ext_own_ref, pot_ref, home_ref,
                fnum_ref, fden_ref, bnum_ref, bden_ref, rows_ref, cols_ref, acc_row, acc_col, mine, other, *ready):
    feat, blocks, tiles_blk = dims
    tiles = blocks * tiles_blk
    held_blk = tiles_blk * SPLITS // blocks
    held = blocks * held_blk
    gain = gain_of(feat)
    progs = fnum_ref.shape[1]
    at_end = lax.axis_index("sec") == lax.axis_size("sec") - 1
    groups = listed_pairs(pairs_ref, counts_ref, mine, other, blocks, tiles_blk, tiles)
    acc_row[...] = jnp.zeros_like(acc_row)
    acc_col[...] = jnp.zeros_like(acc_col)
    for owner in range(blocks):
        for place in range(held_blk):
            start = lane_of(owner, place, blocks)
            rows_ref[:, start : start + WIDTH] = home_ref[owner, place : place + 1, :]
    blk = lax.axis_index("blk")
    for tile in range(tiles_blk):
        here = slice(tile * TILE, (tile + 1) * TILE)
        level = level_ref[pl.ds(blk * tiles_blk + tile, 1), :]
        potential = pot_ref[:, here].astype(jnp.float32) - level * (2.0 / feat)
        cols_ref[:, here] = jnp.where(at_end, 0.0, potential)

    def use(scores, row, col):
        level = level_ref[pl.ds(col, 1), :]
        plan = jnp.exp2((scores[...] - level) * gain).astype(jnp.bfloat16)
        acc_row[row] += lax.dot_general(
            ext_next_ref[col], plan, (((1,), (1,)), ((), ())), preferred_element_type=jnp.float32
        )
        acc_col[col] += jnp.dot(ext_own_ref[row], plan, preferred_element_type=jnp.float32)

    over_pairs(groups, ready, xt_ref, y_ref, mine, other, use)
    for row in range(held):
        owner, place = row // held_blk, row % held_blk
        fnum_ref[owner, :, place * WIDTH : (place + 1) * WIDTH] = acc_row[row, 0:progs, :]
        fden_ref[owner, place : place + 1, :] = acc_row[row, progs : progs + 1, :]
    for col in range(tiles):
        owner, place = col // tiles_blk, col % tiles_blk
        bnum_ref[owner, place] = acc_col[col, 0:progs, :]
        bden_ref[owner, place : place + 1, :] = acc_col[col, progs : progs + 1, :]


def finish_kernel(counts, fnum_ref, fden_ref, bnum_ref, bden_ref, out_ref,
                  hn, hd, an, ad, keep, keep_den, go, go_den, bn, bd, ship, ship_den, cn, cd,
                  send_sem, recv_sem):
    n_sec, blocks = counts
    sec, blk = lax.axis_index("sec"), lax.axis_index("blk")
    tiles_blk = bnum_ref.shape[1]
    held_blk = fden_ref.shape[1]
    kinds = blocks // SPLITS
    has_to, has_from = sec < n_sec - 1, sec > 0
    core, across, corner = mates = mates_of(blk, blocks)
    me, side = blk % 2, blk // 2
    sems = (send_sem, recv_sem)
    greet(
        [(has_to, sec + 1, blk), (has_from, sec - 1, blk)] + [(sec >= 0, sec, mate) for mate in mates]
    )

    def homeward(k, n):
        mate = mates[k]
        src, dst = ((fnum_ref, hn), (fden_ref, hd))[n]
        return send(src.at[mate], dst.at[blk], sems, 2 * k + n, sec, mate)

    steps = tiles_blk + 1
    base = 6

    def pair(t, far):
        place = 1 - side if far else side
        source = 2 * place + 1 - me
        number = base + 2 * t + (0 if far else 1)
        slot = 0 if far else 1
        if t == tiles_blk:
            return send(bden_ref.at[source], ad.at[slot], sems, number, sec, core)
        return send(bnum_ref.at[source, t], an.at[slot, t], sems, number, sec, core)

    def cross(t):
        number = base + 2 * steps + t
        if t == tiles_blk:
            return send(go_den, bd, sems, number, sec, across)
        return send(go.at[t], bn.at[t], sems, number, sec, across)

    def onward(t):
        number = base + 3 * steps + t
        if t == tiles_blk:
            return send(ship_den, cd, sems, number, sec + 1, blk)
        return send(ship.at[t], cn.at[t], sems, number, sec + 1, blk)

    order = [tiles_blk] + list(range(tiles_blk))

    @pl.when(has_to)
    def _():
        for t in order:
            pair(t, True).start()
        for t in order:
            pair(t, False).start()

    hn[blk] = fnum_ref[blk]
    hd[blk] = fden_ref[blk]
    far, near = 2 * (1 - side) + me, 2 * side + me

    @pl.when(has_to)
    def _():
        for t in order:
            pair(t, True).wait_recv()
            if t == tiles_blk:
                go_den[...] = bden_ref[far] + ad[0]
            else:
                go[t] = (bnum_ref[far, t] + an[0, t]).astype(jnp.bfloat16)
            cross(t).start()

    for k in (1, 2, 0):
        for n in range(2):
            homeward(k, n).start()

    @pl.when(has_to)
    def _():
        for t in order:
            pair(t, False).wait_recv()
            if t == tiles_blk:
                keep_den[...] = bden_ref[near] + ad[1]
            else:
                keep[t] = bnum_ref[near, t] + an[1, t]
        for t in order:
            cross(t).wait_recv()
            if t == tiles_blk:
                ship_den[...] = keep_den[...] + bd[...]
            else:
                ship[t] = (keep[t] + bn[t].astype(jnp.float32)).astype(jnp.bfloat16)
            onward(t).start()

    for k in range(3):
        for n in range(2):
            homeward(k, n).wait_recv()

    @pl.when(jnp.logical_not(has_from))
    def _():
        cn[...] = jnp.zeros_like(cn)
        cd[...] = jnp.zeros_like(cd)

    for t in order:

        @pl.when(has_from)
        def _():
            onward(t).wait_recv()

        if t == tiles_blk:
            continue
        place, kind = t // kinds, t % kinds
        owners = [kind * SPLITS + n for n in range(SPLITS)]
        here = slice(place * WIDTH, (place + 1) * WIDTH)
        for n, owner in enumerate(owners):
            part = slice(n * WIDTH, (n + 1) * WIDTH)
            number = hn[owner, :, here] + cn[t, :, part].astype(jnp.float32)
            weight = hd[owner, place : place + 1, :] + cd[t : t + 1, part]
            start = t * TILE + n * WIDTH
            out_ref[:, start : start + WIDTH] = (number / weight).astype(jnp.bfloat16)

    for k in range(3):
        for n in range(2):
            homeward(k, n).wait_send()

    @pl.when(has_to)
    def _():
        for t in range(steps):
            pair(t, True).wait_send()
            pair(t, False).wait_send()
            cross(t).wait_send()
            onward(t).wait_send()


def exchange(kernel, number, out_shape, operands, scratch, space=pltpu.VMEM):
    outs = jax.tree.map(lambda _: pl.BlockSpec(memory_space=pltpu.VMEM), out_shape)
    return pl.pallas_call(
        kernel, out_shape=out_shape, in_specs=[pl.BlockSpec(memory_space=space)] * len(operands),
        out_specs=outs, scratch_shapes=scratch,
        compiler_params=pltpu.CompilerParams(
            collective_id=number, has_side_effects=True, vmem_limit_bytes=VMEM_LIMIT
        ),
    )(*operands)


def call(kernel, out_shape, operands, scratch):
    outs = jax.tree.map(lambda _: pl.BlockSpec(memory_space=pltpu.VMEM), out_shape)
    return pl.pallas_call(
        kernel, out_shape=out_shape,
        in_specs=[pl.BlockSpec(memory_space=pltpu.SMEM)] * 2
        + [pl.BlockSpec(memory_space=pltpu.VMEM)] * (len(operands) - 2),
        out_specs=outs, scratch_shapes=scratch,
        compiler_params=pltpu.CompilerParams(vmem_limit_bytes=VMEM_LIMIT),
    )(*operands)


def body(features, programs, column_pot, tile_pairs, pair_counts):
    feat, cells_blk = features.shape[1:]
    progs = programs.shape[1]
    tiles_blk = cells_blk // TILE
    most = tile_pairs.shape[2]
    blocks, n_sec = lax.axis_size("blk"), lax.axis_size("sec")
    tiles = tiles_blk * blocks
    held_blk = tiles_blk * SPLITS // blocks
    held = blocks * held_blk
    dims = (feat, blocks, tiles_blk)
    counts = (n_sec, blocks)
    depth, ext = depth_of(feat), ext_of(progs)
    f32, bf16, i32 = jnp.float32, jnp.bfloat16, jnp.int32
    shape, vmem = jax.ShapeDtypeStruct, pltpu.VMEM

    def dma(number):
        return [pltpu.SemaphoreType.DMA((number,))] * 2

    mate_copies = (blocks - 1) * (2 * held_blk + 3)
    xt, y, sq, ext_next, ext_own, pairs, all_counts = exchange(
        functools.partial(gather_kernel, counts), 0,
        (
            shape((held, WIDTH, depth), bf16),
            shape((tiles + 1, depth, TILE), bf16),
            shape((blocks, held_blk, WIDTH), f32),
            shape((tiles + 1, ext, TILE), bf16),
            shape((held, ext, WIDTH), bf16),
            shape((blocks, 2, 1, most), i32),
            shape((blocks, 1, 1), i32),
        ),
        [pltpu.with_memory_space_constraint(part, pltpu.HBM) for part in (features[0], programs[0], column_pot, tile_pairs)] + [pair_counts],
        [
            vmem((blocks, feat, cells_blk), bf16),
            vmem((blocks, progs, cells_blk), bf16),
            vmem((blocks, held_blk, feat, WIDTH), bf16),
            vmem((blocks, held_blk, progs, WIDTH), bf16),
            vmem((blocks, 1, cells_blk), bf16),
            vmem((depth, WIDTH), f32),
            *dma(4 * (FEAT_CHUNKS + PROG_CHUNKS)), *dma(mate_copies), pltpu.SemaphoreType.DMA((2 * held_blk + 3,)),
        ],
        pltpu.HBM,
    )
    index = pltpu.SMEM((blocks * most + 2 * UNROLL,), i32)
    ready = [vmem((WIDTH, TILE), f32)] * UNROLL
    pots = shape((blocks, held_blk, WIDTH), f32)
    rp, xt2, cl = call(
        functools.partial(stats_kernel, dims),
        (pots, shape((held, WIDTH, depth), bf16), shape((tiles, TILE), f32)),
        (pairs, all_counts, xt, y, sq),
        [
            vmem((held, WIDTH, LANES), f32), vmem((held, WIDTH, LANES), f32),
            vmem((tiles + 1, 8, TILE), f32), vmem((tiles + 1, 8, TILE), f32), index, index, *ready,
        ],
    )
    level, home = exchange(
        functools.partial(merge_kernel, counts, feat), 1, (shape((tiles + 8, TILE), f32), pots), (rp, cl),
        [vmem((blocks, tiles, TILE), f32), *dma(2 * (blocks - 1))],
    )
    line = shape((1, cells_blk), f32)
    fnum, fden, bnum, bden, row_out, col_out = call(
        functools.partial(plan_kernel, dims),
        (
            shape((blocks, progs, held_blk * WIDTH), f32), pots,
            shape((blocks, tiles_blk, progs, TILE), f32), shape((blocks, tiles_blk, TILE), f32), line, line,
        ),
        (pairs, all_counts, xt2, y, level, ext_next, ext_own, column_pot, home),
        [vmem((held, ext, WIDTH), f32), vmem((tiles + 1, ext, TILE), f32), index, index, *ready],
    )
    num, den = vmem((tiles_blk, progs, TILE), bf16), vmem((tiles_blk, TILE), f32)
    smoothed = exchange(
        functools.partial(finish_kernel, counts), 2, shape((progs, cells_blk), bf16), (fnum, fden, bnum, bden),
        [
            vmem((blocks, progs, held_blk * WIDTH), f32), vmem((blocks, held_blk, WIDTH), f32),
            vmem((2, tiles_blk, progs, TILE), f32), vmem((2, tiles_blk, TILE), f32),
            vmem((tiles_blk, progs, TILE), f32), den, num, den, num, den, num, den, num, den,
            *dma(6 + 4 * (tiles_blk + 1)),
        ],
    )
    return smoothed[None], row_out, col_out


def solution(mesh):
    in_specs = (
        P("sec", None, "blk"),
        P("sec", None, "blk"),
        P("sec", "blk"),
        P(None, "sec", "blk"),
        P("sec", "blk"),
    )
    out_specs = (P("sec", None, "blk"), P("sec", "blk"), P("sec", "blk"))
    return jax.shard_map(body, mesh=mesh, in_specs=in_specs, out_specs=out_specs, check_vma=False)
```

```python
import functools
import math

import jax
import jax.numpy as jnp
from jax import lax
from jax.experimental import pallas as pl
from jax.experimental.pallas import tpu as pltpu
from jax.sharding import PartitionSpec as P

TILE = 512
EPSILON = 0.05
LOG2E = math.log2(math.e)
NEG = -1e30
UNROLL = 4
SPLITS = 2
WIDTH = TILE // SPLITS
LANES = 128
VMEM_LIMIT = 24 << 20
MESH = pl.DeviceIdType.MESH


def depth_of(feat):
    return -(-(feat + 8) // 16) * 16


def ext_of(progs):
    return -(-(progs + 1) // 16) * 16


def gain_of(feat):
    return 2.0 * LOG2E / (feat * EPSILON)


def split3(value):
    hi = value.astype(jnp.bfloat16).astype(jnp.float32)
    rest = value - hi
    mid = rest.astype(jnp.bfloat16).astype(jnp.float32)
    return hi, mid, rest - mid


def lists_width(blocks, most):
    return -(-(blocks * most + 3 * UNROLL) // LANES) * LANES


def rows_of(pieces, width):
    index = lax.broadcasted_iota(jnp.int32, (8, width), 0)
    block = jnp.zeros((8, width), jnp.float32)
    for place, piece in enumerate(pieces):
        block = jnp.where(index == place, piece, block)
    return block


def sum_squares(cells):
    return jnp.sum(cells * cells, axis=0, keepdims=True)


def lane_of(owner, place, blocks):
    kinds = blocks // SPLITS
    return (place * kinds + owner // SPLITS) * TILE + (owner % SPLITS) * WIDTH


def greet(targets):
    barrier = pltpu.get_barrier_semaphore()
    expected = jnp.int32(0)
    for used, sec, blk in targets:

        @pl.when(used)
        def _():
            pl.semaphore_signal(barrier, inc=1, device_id=(sec, blk), device_id_type=MESH)

        expected = expected + jnp.where(used, 1, 0)
    pl.semaphore_wait(barrier, expected)


def send(src, dst, sems, place, sec, blk):
    return pltpu.make_async_remote_copy(
        src_ref=src, dst_ref=dst, send_sem=sems[0].at[place], recv_sem=sems[1].at[place],
        device_id=(sec, blk), device_id_type=MESH,
    )


def mates_of(blk, blocks):
    core = blk + 1 - 2 * (blk % 2)
    across = (blk + 2) % blocks
    corner = core + 2 - 4 * (core // 2)
    return core, across, corner


def ext_tail(progs, width):
    index = lax.broadcasted_iota(jnp.int32, (ext_of(progs) - progs, width), 0)
    return jnp.where(index == 0, 1.0, 0.0).astype(jnp.bfloat16)


FEAT_CHUNKS = 4
PARTS = 1


def compact_lists(pairs_ref, counts_ref, lists_ref, kind, blocks, tiles_blk):
    most = pairs_ref.shape[3]
    width = lists_ref.shape[1]
    kinds = blocks // SPLITS
    tiles = blocks * tiles_blk
    f32, bf16 = jnp.float32, jnp.bfloat16
    slot = lax.broadcasted_iota(jnp.int32, (1, most), 1)
    before = lax.broadcasted_iota(jnp.int32, (most, most), 0) < lax.broadcasted_iota(jnp.int32, (most, most), 1)
    before = jnp.where(before, 1.0, 0.0).astype(bf16)
    spot = lax.broadcasted_iota(jnp.int32, (width, most), 0).astype(f32)
    line = lax.broadcasted_iota(jnp.int32, (8, most), 0)
    start = jnp.full((1, 1), UNROLL, f32)
    found = jnp.zeros((8, width), f32)
    for block in range(blocks):
        row = pairs_ref[block, 0] + block * tiles_blk
        keep = jnp.logical_and(slot < counts_ref[block], row % kinds == kind)
        flag = jnp.where(keep, 1.0, 0.0)
        flags = jnp.broadcast_to(flag, (8, most))
        rank = jnp.dot(flags.astype(bf16), before, preferred_element_type=f32)[0:1] + start
        hits = jnp.where(keep, jnp.where(spot == rank, 1.0, 0.0), 0.0).astype(bf16)
        held, across = (row // kinds).astype(f32), pairs_ref[block, 1].astype(f32)
        values = jnp.where(line == 0, held, jnp.where(line == 1, across, 1.0)).astype(bf16)
        found += lax.dot_general(values, hits, (((1,), (1,)), ((), ())), preferred_element_type=f32)
        start = start + jnp.sum(flag, axis=1, keepdims=True)
    index = lax.broadcasted_iota(jnp.int32, (8, width), 0)
    other = jnp.where(found[2:3] > 0.0, found[1:2], float(tiles))
    table = jnp.where(index == 0, found[0:1], jnp.where(index == 1, other, start - UNROLL))
    lists_ref[...] = table.astype(jnp.int32)


def gather_kernel(counts, x_ref, prog_ref, pot_ref, pair_ref, count_ref,
                  xrec_ref, y_ref, yt_ref, sq_ref, pack_ref, pown_ref, lists_ref,
                  xs, own_x, pots, pairs, pair_counts, xbuild, ybuild,
                  send_sem, recv_sem, mate_send, mate_recv, local_sem):
    n_sec, blocks = counts
    sec, blk = lax.axis_index("sec"), lax.axis_index("blk")
    feat, cells_blk = x_ref.shape
    depth = depth_of(feat)
    aux = depth - 8
    gain = gain_of(feat)
    tiles_blk = cells_blk // TILE
    tiles = tiles_blk * blocks
    held_blk = tiles_blk * SPLITS // blocks
    piece = held_blk * WIDTH
    has_to, has_from = sec > 0, sec < n_sec - 1
    core, across, corner = mates = mates_of(blk, blocks)
    me = blk % 2
    mine_at = pl.multiple_of(me * cells_blk, LANES)
    beside_at = pl.multiple_of(SPLITS * cells_blk + me * piece, LANES)
    own_at = pl.multiple_of(me * piece, LANES)

    def prog_piece(owner, place):
        return prog_ref.at[:, pl.ds(pl.multiple_of(lane_of(owner, place, blocks), WIDTH), WIDTH)]

    moves = [(pot_ref, pots.at[blk]), (pair_ref, pairs.at[blk]), (count_ref, pair_counts.at[blk])]
    for place in range(held_blk):
        start = pl.multiple_of(lane_of(blk, place, blocks), WIDTH)
        moves.append((x_ref.at[:, pl.ds(start, WIDTH)], own_x.at[blk, place]))
    for place in range(held_blk):
        moves.append((prog_piece(blk, place), pown_ref.at[:, pl.ds(own_at + place * WIDTH, WIDTH)]))
        moves.append((prog_piece(across, place), pack_ref.at[:, pl.ds(beside_at + place * WIDTH, WIDTH)]))
    locals_ = [pltpu.make_async_copy(src, dst, local_sem.at[n]) for n, (src, dst) in enumerate(moves)]
    for copy in locals_:
        copy.start()
    greet(
        [(has_to, sec - 1, blk), (has_from, sec + 1, blk)] + [(sec >= 0, sec, mate) for mate in mates]
    )
    sems, mate_sems = (send_sem, recv_sem), (mate_send, mate_recv)
    feat_step = cells_blk // FEAT_CHUNKS
    chunks = [(n * feat_step, feat_step) for n in range(FEAT_CHUNKS)]
    last = 4 * len(chunks)

    def first(c):
        start, size = chunks[c]
        return send(
            x_ref.at[:, start : start + size], xs.at[blk, :, start : start + size], sems, 4 * c, sec - 1, blk
        )

    def first_programs():
        return send(prog_ref, pack_ref.at[:, pl.ds(mine_at, cells_blk)], sems, last, sec - 1, blk)

    def share_programs():
        slot = pack_ref.at[:, pl.ds(mine_at, cells_blk)]
        return send(slot, slot, sems, last + 1, sec, core)

    def share(c, kind):
        start, size = chunks[c]
        slot = xs.at[across if kind == 2 else blk, :, start : start + size]
        return send(slot, slot, sems, 4 * c + 1 + kind, sec, across if kind == 0 else core)

    def to_mate(k):
        mate = mates[k]
        copies = [(pot_ref, pots.at[blk]), (pair_ref, pairs.at[blk]), (count_ref, pair_counts.at[blk])]
        for place in range(held_blk):
            start = pl.multiple_of(lane_of(mate, place, blocks), WIDTH)
            copies.append((x_ref.at[:, pl.ds(start, WIDTH)], own_x.at[blk, place]))
        per = len(copies)
        return [send(src, dst, mate_sems, per * k + n, sec, mate) for n, (src, dst) in enumerate(copies)]

    def pieces_to_core():
        base = 3 * (held_blk + 3)
        copies = []
        for place in range(held_blk):
            copies.append((prog_piece(core, place), pown_ref.at[:, pl.ds(own_at + place * WIDTH, WIDTH)]))
            copies.append((prog_piece(corner, place), pack_ref.at[:, pl.ds(beside_at + place * WIDTH, WIDTH)]))
        return [send(src, dst, mate_sems, base + n, sec, core) for n, (src, dst) in enumerate(copies)]

    @pl.when(has_to)
    def _():
        for c in range(len(chunks)):
            first(c).start()
        first_programs().start()

    to_mates = [to_mate(k) for k in range(3)]
    for n in range(len(to_mates[0])):
        for k in (1, 2, 0):
            to_mates[k][n].start()
    to_core = pieces_to_core()
    for copy in to_core:
        copy.start()

    xbuild[...] = jnp.zeros_like(xbuild)
    xbuild[aux:depth, :] = rows_of([1.0] * 3, WIDTH)
    ybuild[...] = jnp.zeros_like(ybuild)
    row = lax.broadcasted_iota(jnp.int32, y_ref.shape[1:], 0)
    y_ref[tiles] = jnp.where(row == aux, NEG, 0.0).astype(jnp.bfloat16)
    lane = lax.broadcasted_iota(jnp.int32, yt_ref.shape[1:], 1)
    yt_ref[tiles] = jnp.where(lane == aux, NEG, 0.0).astype(jnp.bfloat16)
    for copy in locals_:
        copy.wait()

    def build_own(owner):
        for place in range(held_blk):
            cells = own_x[owner, place].astype(jnp.float32)
            scaled = cells * gain
            high = scaled.astype(jnp.bfloat16).astype(jnp.float32)
            xbuild[0:feat, :] = high
            xbuild[depth : depth + feat, :] = scaled - high
            xrec_ref[owner * held_blk + place] = xbuild[...].astype(jnp.bfloat16)
            sq_ref[owner, place : place + 1, :] = sum_squares(cells)

    ones = jnp.ones((1, TILE), jnp.float32)

    def build_next(owner, c):
        begin, size = chunks[c]
        for start in range(begin, begin + size, TILE):
            tile = owner * tiles_blk + start // TILE
            cells = xs[owner, :, start : start + TILE].astype(jnp.float32)
            pot = pots[owner, :, start : start + TILE].astype(jnp.float32)
            bias = pot * (LOG2E / EPSILON) - sum_squares(cells) * (gain * 0.5)
            ybuild[0:feat, :] = cells
            ybuild[depth : depth + feat, :] = cells
            ybuild[aux:depth, :] = rows_of(split3(bias) + (ones,) * 3, TILE)
            y_ref[tile] = ybuild[...].astype(jnp.bfloat16)
            yt_ref[tile] = ybuild[...].T.astype(jnp.bfloat16)

    for k in range(3):
        for copy in to_mates[k][:3]:
            copy.wait_recv()
    compact_lists(pairs, pair_counts, lists_ref, blk // SPLITS, blocks, tiles_blk)
    build_own(blk)

    @pl.when(has_from)
    def _():
        for turn in range(len(chunks) + 2):
            if turn < len(chunks):
                first(turn).wait_recv()
                share(turn, 0).start()
                share(turn, 1).start()
                build_next(blk, turn)
            if 0 <= turn - 1 < len(chunks):
                share(turn - 1, 0).wait_recv()
                share(turn - 1, 2).start()
                build_next(across, turn - 1)
                share(turn - 1, 1).wait_recv()
                build_next(core, turn - 1)
            if turn == len(chunks):
                first_programs().wait_recv()
                share_programs().start()
            if 0 <= turn - 2 < len(chunks):
                share(turn - 2, 2).wait_recv()
                build_next(corner, turn - 2)
        share_programs().wait_recv()

    @pl.when(jnp.logical_not(has_from))
    def _():
        pack_ref[:, 0 : SPLITS * cells_blk] = jnp.zeros((pack_ref.shape[0], SPLITS * cells_blk), jnp.bfloat16)

    for k, mate in enumerate(mates):
        for copy in to_mates[k][3:]:
            copy.wait_recv()
        build_own(mate)
    for copy in to_core:
        copy.wait_recv()

    @pl.when(has_to)
    def _():
        for c in range(len(chunks)):
            first(c).wait_send()
        first_programs().wait_send()

    @pl.when(has_from)
    def _():
        for c in range(len(chunks)):
            for kind in range(3):
                share(c, kind).wait_send()
        share_programs().wait_send()

    for k in range(3):
        for copy in to_mates[k]:
            copy.wait_send()
    for copy in to_core:
        copy.wait_send()


def rounds_of(lists_ref):
    return (lists_ref[2, 0] + UNROLL - 1) // UNROLL


def stats_kernel(dims, lists_ref, xrec_ref, y_ref, yt_ref, sq_ref, rp_ref, xt_out, cl_ref,
                 top_row, sum_row, top_col, sum_col, tops_row, tops_col, *ready):
    feat, blocks, tiles_blk = dims
    tiles = blocks * tiles_blk
    held_blk = tiles_blk * SPLITS // blocks
    held = blocks * held_blk
    half_gain = gain_of(feat) * 0.5
    depth = depth_of(feat)
    aux = depth - 8
    at_end = lax.axis_index("sec") == lax.axis_size("sec") - 1
    rounds = rounds_of(lists_ref)
    for ref in (top_row, top_col):
        ref[...] = jnp.full_like(ref, NEG)
    for ref in (sum_row, sum_col):
        ref[...] = jnp.zeros_like(ref)

    def sweep(scores_of, ready, tops, top_acc, sum_acc, by_row):
        rows, width = ready[0].shape
        size = rows // PARTS

        def make(at, slot):
            best = None
            for start in range(0, rows, size):
                here = pl.ds(start, size)
                scores = scores_of(lists_ref[0, at], lists_ref[1, at], here)
                ready[slot][here, :] = scores
                found = jnp.max(scores.reshape(size // 8, 8, width), axis=0)
                best = found if best is None else jnp.maximum(best, found)
            tops[slot] = best

        def use(at, slot):
            target = lists_ref[0 if by_row else 1, at]
            old = top_acc[target]
            new = jnp.maximum(old, tops[slot])
            total = sum_acc[target] * jnp.exp2(old - new)
            for start in range(0, rows, size):
                scores = ready[slot][start : start + size, :].reshape(size // 8, 8, width)
                total = total + jnp.sum(jnp.exp2(scores - new[None]), axis=0)
            sum_acc[target] = total
            top_acc[target] = new

        for n in range(UNROLL):
            make(UNROLL + n, n)

        def step(index, carry):
            for n in range(UNROLL):
                at = index * UNROLL + UNROLL + n
                use(at, n)
                make(at + UNROLL, n)
            return carry

        lax.fori_loop(0, rounds, step, 0)

    def level_of(tops, sums):
        top = jnp.max(tops, axis=0, keepdims=True)
        total = jnp.sum(sums * jnp.exp2(tops - top), axis=0, keepdims=True)
        return top, total

    sweep(
        lambda row, col, here: jnp.dot(yt_ref[col, here, :], xrec_ref[row], preferred_element_type=jnp.float32),
        ready[:UNROLL], tops_row, top_row, sum_row, True,
    )
    record_row = lax.broadcasted_iota(jnp.int32, (8, WIDTH), 0)
    for row in range(held):
        owner, place = row // held_blk, row % held_blk
        top, total = level_of(top_row[row], sum_row[row])
        level = top + jnp.log2(total)
        potential = (sq_ref[owner, place : place + 1, :] * half_gain - level) * (EPSILON / LOG2E)
        rp_ref[owner, place : place + 1, :] = jnp.where(at_end, 0.0, potential)
        extra = rows_of((1.0,) * 3 + split3(-level), WIDTH)
        record = xrec_ref[row].astype(jnp.float32)
        record = jnp.concatenate([record[0:aux], extra, record[depth:]], axis=0)
        xt_out[row] = record.T.astype(jnp.bfloat16)
    sweep(
        lambda row, col, here: jnp.dot(xt_out[row, here, :], y_ref[col], preferred_element_type=jnp.float32),
        ready[UNROLL:], tops_col, top_col, sum_col, False,
    )
    for col in range(tiles):
        top, total = level_of(top_col[col], sum_col[col])
        cl_ref[col : col + 1, :] = jnp.where(total > 0.0, top + jnp.log2(total), NEG)


def merge_kernel(counts, rp_ref, cl_ref, level_ref, home_ref, parts, send_sem, recv_sem):
    n_sec, blocks = counts
    sec, blk = lax.axis_index("sec"), lax.axis_index("blk")
    tiles = cl_ref.shape[0]
    mates = mates_of(blk, blocks)
    sems = (send_sem, recv_sem)
    greet([(sec >= 0, sec, mate) for mate in mates])
    copies = []
    for k, mate in enumerate(mates):
        copies.append(send(cl_ref, parts.at[blk], sems, 2 * k, sec, mate))
        copies.append(send(rp_ref.at[mate], home_ref.at[blk], sems, 2 * k + 1, sec, mate))
    for k in (1, 2, 0):
        for copy in copies[2 * k : 2 * k + 2]:
            copy.start()
    parts[blk] = cl_ref[...]
    home_ref[blk] = rp_ref[blk]
    level_ref[tiles:, :] = jnp.zeros((level_ref.shape[0] - tiles, TILE), jnp.float32)
    for copy in copies:
        copy.wait_recv()
    levels = [parts[n] for n in range(blocks)]
    top = functools.reduce(jnp.maximum, levels)
    total = functools.reduce(jnp.add, [jnp.exp2(level - top) for level in levels])
    level_ref[0:tiles, :] = top + jnp.log2(total)
    for copy in copies:
        copy.wait_send()


def plan_kernel(dims, lists_ref, xt_ref, y_ref, level_ref, near_ref, pown_ref, far_ref, pot_ref, home_ref,
                fnum_ref, fden_ref, bnum_ref, bden_ref, rows_ref, cols_ref,
                acc_row, acc_col, ext_next_ref, ext_own_ref, *ready):
    feat, blocks, tiles_blk = dims
    tiles = blocks * tiles_blk
    held_blk = tiles_blk * SPLITS // blocks
    held = blocks * held_blk
    cells_blk = tiles_blk * TILE
    piece = held_blk * WIDTH
    progs = fnum_ref.shape[1]
    kept = acc_row.shape[1]
    at_end = lax.axis_index("sec") == lax.axis_size("sec") - 1
    blk = lax.axis_index("blk")
    side = blk // SPLITS
    rounds = rounds_of(lists_ref)
    scores, plans = ready[:UNROLL], ready[UNROLL:]

    def make(at, place):
        scores[place][...] = jnp.dot(
            xt_ref[lists_ref[0, at]], y_ref[lists_ref[1, at]], preferred_element_type=jnp.float32
        )

    for n in range(UNROLL):
        make(UNROLL + n, n)
        plans[n][...] = jnp.zeros_like(plans[n])
    acc_row[...] = jnp.zeros_like(acc_row)
    acc_col[...] = jnp.zeros_like(acc_col)
    ext_next_ref[tiles] = jnp.zeros(ext_next_ref.shape[1:], jnp.bfloat16)
    for group, nums, owns, shift in ((side, near_ref, pown_ref, 0), (1 - side, far_ref, far_ref, SPLITS * cells_blk)):
        for n in range(SPLITS):
            owner = group * SPLITS + n
            for tile in range(tiles_blk):
                start = n * cells_blk + tile * TILE
                ext_next_ref[owner * tiles_blk + tile, 0:progs, :] = nums[:, start : start + TILE]
                ext_next_ref[owner * tiles_blk + tile, progs:, :] = ext_tail(progs, TILE)
            for place in range(held_blk):
                start = shift + n * piece + place * WIDTH
                ext_own_ref[owner * held_blk + place, 0:progs, :] = owns[:, start : start + WIDTH]
                ext_own_ref[owner * held_blk + place, progs:, :] = ext_tail(progs, WIDTH)
    for owner in range(blocks):
        for place in range(held_blk):
            start = lane_of(owner, place, blocks)
            rows_ref[:, start : start + WIDTH] = home_ref[owner, place : place + 1, :]
    for tile in range(tiles_blk):
        here = slice(tile * TILE, (tile + 1) * TILE)
        level = level_ref[pl.ds(blk * tiles_blk + tile, 1), :]
        potential = pot_ref[:, here].astype(jnp.float32) - level * (EPSILON / LOG2E)
        cols_ref[:, here] = jnp.where(at_end, 0.0, potential)

    def weigh(at, place):
        level = level_ref[pl.ds(lists_ref[1, at], 1), :]
        plans[place][...] = jnp.exp2(scores[place][...] - level).astype(jnp.bfloat16)

    def gather(at, place):
        row, col = lists_ref[0, at], lists_ref[1, at]
        plan = plans[place][...]
        acc_row[row] += lax.dot_general(
            ext_next_ref[col], plan, (((1,), (1,)), ((), ())), preferred_element_type=jnp.float32
        )[0:kept]
        acc_col[col] += jnp.dot(ext_own_ref[row], plan, preferred_element_type=jnp.float32)[0:kept]

    def step(index, carry):
        for n in range(UNROLL):
            at = index * UNROLL + UNROLL + n
            gather(at - UNROLL, n)
            weigh(at, n)
            make(at + UNROLL, n)
        return carry

    lax.fori_loop(0, rounds, step, 0)
    for n in range(UNROLL):
        gather(rounds * UNROLL + n, n)
    for row in range(held):
        owner, place = row // held_blk, row % held_blk
        fnum_ref[owner, :, place * WIDTH : (place + 1) * WIDTH] = acc_row[row, 0:progs, :]
        fden_ref[owner, place : place + 1, :] = acc_row[row, progs : progs + 1, :]
    for col in range(tiles):
        owner, place = col // tiles_blk, col % tiles_blk
        bnum_ref[owner, place] = acc_col[col, 0:progs, :]
        bden_ref[owner, place : place + 1, :] = acc_col[col, progs : progs + 1, :]


def finish_kernel(counts, fnum_ref, fden_ref, bnum_ref, bden_ref, out_ref,
                  hn, hd, an, ad, keep, keep_den, go, go_den, bn, bd, ship, ship_den, cn, cd,
                  send_sem, recv_sem):
    n_sec, blocks = counts
    sec, blk = lax.axis_index("sec"), lax.axis_index("blk")
    tiles_blk = bnum_ref.shape[1]
    held_blk = fden_ref.shape[1]
    kinds = blocks // SPLITS
    has_to, has_from = sec < n_sec - 1, sec > 0
    core, across, corner = mates = mates_of(blk, blocks)
    me, side = blk % 2, blk // 2
    sems = (send_sem, recv_sem)
    greet(
        [(has_to, sec + 1, blk), (has_from, sec - 1, blk)] + [(sec >= 0, sec, mate) for mate in mates]
    )

    def homeward(k, n):
        mate = mates[k]
        src, dst = ((fnum_ref, hn), (fden_ref, hd))[n]
        return send(src.at[mate], dst.at[blk], sems, 2 * k + n, sec, mate)

    steps = tiles_blk + 1
    base = 6

    def pair(t, far):
        place = 1 - side if far else side
        source = 2 * place + 1 - me
        number = base + 2 * t + (0 if far else 1)
        slot = 0 if far else 1
        if t == tiles_blk:
            return send(bden_ref.at[source], ad.at[slot], sems, number, sec, core)
        return send(bnum_ref.at[source, t], an.at[slot, t], sems, number, sec, core)

    def cross(t):
        number = base + 2 * steps + t
        if t == tiles_blk:
            return send(go_den, bd, sems, number, sec, across)
        return send(go.at[t], bn.at[t], sems, number, sec, across)

    def onward(t):
        number = base + 3 * steps + t
        if t == tiles_blk:
            return send(ship_den, cd, sems, number, sec + 1, blk)
        return send(ship.at[t], cn.at[t], sems, number, sec + 1, blk)

    order = [tiles_blk] + list(range(tiles_blk))

    @pl.when(has_to)
    def _():
        for t in order:
            pair(t, True).start()
        for t in order:
            pair(t, False).start()

    hn[blk] = fnum_ref[blk]
    hd[blk] = fden_ref[blk]
    far, near = 2 * (1 - side) + me, 2 * side + me

    @pl.when(has_to)
    def _():
        for t in order:
            pair(t, True).wait_recv()
            if t == tiles_blk:
                go_den[...] = bden_ref[far] + ad[0]
            else:
                go[t] = (bnum_ref[far, t] + an[0, t]).astype(jnp.bfloat16)
            cross(t).start()

    for k in (1, 2, 0):
        for n in range(2):
            homeward(k, n).start()

    @pl.when(has_to)
    def _():
        for t in order:
            pair(t, False).wait_recv()
            if t == tiles_blk:
                keep_den[...] = bden_ref[near] + ad[1]
            else:
                keep[t] = bnum_ref[near, t] + an[1, t]
        for t in order:
            cross(t).wait_recv()
            if t == tiles_blk:
                ship_den[...] = keep_den[...] + bd[...]
            else:
                ship[t] = (keep[t] + bn[t].astype(jnp.float32)).astype(jnp.bfloat16)
            onward(t).start()

    for k in range(3):
        for n in range(2):
            homeward(k, n).wait_recv()

    @pl.when(jnp.logical_not(has_from))
    def _():
        cn[...] = jnp.zeros_like(cn)
        cd[...] = jnp.zeros_like(cd)

    for t in order:

        @pl.when(has_from)
        def _():
            onward(t).wait_recv()

        if t == tiles_blk:
            continue
        place, kind = t // kinds, t % kinds
        owners = [kind * SPLITS + n for n in range(SPLITS)]
        here = slice(place * WIDTH, (place + 1) * WIDTH)
        for n, owner in enumerate(owners):
            part = slice(n * WIDTH, (n + 1) * WIDTH)
            number = hn[owner, :, here] + cn[t, :, part].astype(jnp.float32)
            weight = hd[owner, place : place + 1, :] + cd[t : t + 1, part]
            start = t * TILE + n * WIDTH
            out_ref[:, start : start + WIDTH] = (number / weight).astype(jnp.bfloat16)

    for k in range(3):
        for n in range(2):
            homeward(k, n).wait_send()

    @pl.when(has_to)
    def _():
        for t in range(steps):
            pair(t, True).wait_send()
            pair(t, False).wait_send()
            cross(t).wait_send()
            onward(t).wait_send()


def exchange(kernel, number, out_shape, operands, scratch, space=pltpu.VMEM):
    outs = jax.tree.map(lambda _: pl.BlockSpec(memory_space=pltpu.VMEM), out_shape)
    return pl.pallas_call(
        kernel, out_shape=out_shape, in_specs=[pl.BlockSpec(memory_space=space)] * len(operands),
        out_specs=outs, scratch_shapes=scratch,
        compiler_params=pltpu.CompilerParams(
            collective_id=number, has_side_effects=True, vmem_limit_bytes=VMEM_LIMIT
        ),
    )(*operands)


def call(kernel, out_shape, operands, scratch):
    outs = jax.tree.map(lambda _: pl.BlockSpec(memory_space=pltpu.VMEM), out_shape)
    return pl.pallas_call(
        kernel, out_shape=out_shape,
        in_specs=[pl.BlockSpec(memory_space=pltpu.SMEM)]
        + [pl.BlockSpec(memory_space=pltpu.VMEM)] * (len(operands) - 1),
        out_specs=outs, scratch_shapes=scratch,
        compiler_params=pltpu.CompilerParams(vmem_limit_bytes=VMEM_LIMIT),
    )(*operands)


def body(features, programs, column_pot, tile_pairs, pair_counts):
    feat, cells_blk = features.shape[1:]
    progs = programs.shape[1]
    tiles_blk = cells_blk // TILE
    most = tile_pairs.shape[2]
    blocks, n_sec = lax.axis_size("blk"), lax.axis_size("sec")
    tiles = tiles_blk * blocks
    held_blk = tiles_blk * SPLITS // blocks
    held = blocks * held_blk
    dims = (feat, blocks, tiles_blk)
    counts = (n_sec, blocks)
    depth, ext = depth_of(feat), ext_of(progs)
    f32, bf16, i32 = jnp.float32, jnp.bfloat16, jnp.int32
    shape, vmem = jax.ShapeDtypeStruct, pltpu.VMEM

    def dma(number):
        return [pltpu.SemaphoreType.DMA((number,))] * 2

    piece = held_blk * WIDTH
    kept = -(-(progs + 1) // 8) * 8
    mate_copies = (blocks - 1) * (held_blk + 3) + 2 * held_blk
    packed = SPLITS * (cells_blk + piece)
    spaced = [
        pltpu.with_memory_space_constraint(part, pltpu.HBM)
        for part in (features[0], programs[0], column_pot, tile_pairs)
    ]
    xrec, y, yt, sq, pack, pown, lists = exchange(
        functools.partial(gather_kernel, counts), 0,
        (
            shape((held, 2 * depth, WIDTH), bf16),
            shape((tiles + 1, 2 * depth, TILE), bf16),
            shape((tiles + 1, TILE, 2 * depth), bf16),
            shape((blocks, held_blk, WIDTH), f32),
            shape((progs, packed), bf16),
            shape((progs, SPLITS * piece), bf16),
            shape((8, lists_width(blocks, most)), i32),
        ),
        (*spaced, pair_counts),
        [
            vmem((blocks, feat, cells_blk), bf16),
            vmem((blocks, held_blk, feat, WIDTH), bf16),
            vmem((blocks, 1, cells_blk), bf16),
            vmem((blocks, 2, 1, most), i32),
            vmem((blocks, 1, 1), i32),
            vmem((2 * depth, WIDTH), f32),
            vmem((2 * depth, TILE), f32),
            *dma(4 * FEAT_CHUNKS + 2), *dma(mate_copies), pltpu.SemaphoreType.DMA((3 + 3 * held_blk,)),
        ],
        pltpu.HBM,
    )
    far = lax.ppermute(pack, "blk", [(source, (source + 2) % blocks) for source in range(blocks)])
    pots = shape((blocks, held_blk, WIDTH), f32)
    tall, wide = vmem((TILE, WIDTH), f32), vmem((WIDTH, TILE), f32)
    rp, xt, cl = call(
        functools.partial(stats_kernel, dims),
        (pots, shape((held, WIDTH, 2 * depth), bf16), shape((tiles, TILE), f32)),
        (lists, xrec, y, yt, sq),
        [
            vmem((held, 8, WIDTH), f32), vmem((held, 8, WIDTH), f32),
            vmem((tiles + 1, 8, TILE), f32), vmem((tiles + 1, 8, TILE), f32),
            vmem((UNROLL, 8, WIDTH), f32), vmem((UNROLL, 8, TILE), f32), *[tall] * UNROLL, *[wide] * UNROLL,
        ],
    )
    level, home = exchange(
        functools.partial(merge_kernel, counts), 1, (shape((tiles + 8, TILE), f32), pots), (rp, cl),
        [vmem((blocks, tiles, TILE), f32), *dma(2 * (blocks - 1))],
    )
    line = shape((1, cells_blk), f32)
    flat = vmem((WIDTH, TILE), bf16)
    fnum, fden, bnum, bden, row_out, col_out = call(
        functools.partial(plan_kernel, dims),
        (
            shape((blocks, progs, held_blk * WIDTH), f32), pots,
            shape((blocks, tiles_blk, progs, TILE), f32), shape((blocks, tiles_blk, TILE), f32), line, line,
        ),
        (lists, xt, y, level, pack, pown, far, column_pot, home),
        [
            vmem((held, kept, WIDTH), f32), vmem((tiles + 1, kept, TILE), f32),
            vmem((tiles + 1, ext, TILE), bf16), vmem((held, ext, WIDTH), bf16), *[wide] * UNROLL, *[flat] * UNROLL,
        ],
    )
    num, den = vmem((tiles_blk, progs, TILE), bf16), vmem((tiles_blk, TILE), f32)
    smoothed = exchange(
        functools.partial(finish_kernel, counts), 2, shape((progs, cells_blk), bf16), (fnum, fden, bnum, bden),
        [
            vmem((blocks, progs, held_blk * WIDTH), f32), vmem((blocks, held_blk, WIDTH), f32),
            vmem((2, tiles_blk, progs, TILE), f32), vmem((2, tiles_blk, TILE), f32),
            vmem((tiles_blk, progs, TILE), f32), den, num, den, num, den, num, den, num, den,
            *dma(6 + 4 * (tiles_blk + 1)),
        ],
    )
    return smoothed[None], row_out, col_out


def solution(mesh):
    in_specs = (
        P("sec", None, "blk"),
        P("sec", None, "blk"),
        P("sec", "blk"),
        P(None, "sec", "blk"),
        P("sec", "blk"),
    )
    out_specs = (P("sec", None, "blk"), P("sec", "blk"), P("sec", "blk"))
    return jax.shard_map(body, mesh=mesh, in_specs=in_specs, out_specs=out_specs, check_vma=False)
```

```python
import functools
import math

import jax
import jax.numpy as jnp
from jax import lax
from jax.experimental import pallas as pl
from jax.experimental.pallas import tpu as pltpu
from jax.sharding import PartitionSpec as P

TILE = 512
EPSILON = 0.05
LOG2E = math.log2(math.e)
NEG = -1e30
UNROLL = 4
SLOTS = 2
SPLITS = 2
WIDTH = TILE // SPLITS
LANES = 128
VMEM_LIMIT = 24 << 20
MESH = pl.DeviceIdType.MESH


def depth_of(feat):
    return -(-(feat + 8) // 16) * 16


def ext_of(progs):
    return -(-(progs + 1) // 16) * 16


def gain_of(feat):
    return 2.0 * LOG2E / (feat * EPSILON)


def split3(value):
    hi = value.astype(jnp.bfloat16).astype(jnp.float32)
    rest = value - hi
    mid = rest.astype(jnp.bfloat16).astype(jnp.float32)
    return hi, mid, rest - mid


def lists_width(blocks, most):
    return -(-(blocks * most + 3 * UNROLL) // LANES) * LANES


def rows_of(pieces, width):
    index = lax.broadcasted_iota(jnp.int32, (8, width), 0)
    block = jnp.zeros((8, width), jnp.float32)
    for place, piece in enumerate(pieces):
        block = jnp.where(index == place, piece, block)
    return block


def sum_squares(cells):
    return jnp.sum(cells * cells, axis=0, keepdims=True)


def lane_of(owner, place, blocks):
    kinds = blocks // SPLITS
    return (place * kinds + owner // SPLITS) * TILE + (owner % SPLITS) * WIDTH


def greet(targets):
    barrier = pltpu.get_barrier_semaphore()
    expected = jnp.int32(0)
    for used, sec, blk in targets:

        @pl.when(used)
        def _():
            pl.semaphore_signal(barrier, inc=1, device_id=(sec, blk), device_id_type=MESH)

        expected = expected + jnp.where(used, 1, 0)
    pl.semaphore_wait(barrier, expected)


def send(src, dst, sems, place, sec, blk):
    return pltpu.make_async_remote_copy(
        src_ref=src, dst_ref=dst, send_sem=sems[0].at[place], recv_sem=sems[1].at[place],
        device_id=(sec, blk), device_id_type=MESH,
    )


def mates_of(blk, blocks):
    core = blk + 1 - 2 * (blk % 2)
    across = (blk + 2) % blocks
    corner = core + 2 - 4 * (core // 2)
    return core, across, corner


def ext_tail(progs, width):
    index = lax.broadcasted_iota(jnp.int32, (ext_of(progs) - progs, width), 0)
    return jnp.where(index == 0, 1.0, 0.0).astype(jnp.bfloat16)


FEAT_CHUNKS = 4
LAG = 3
PARTS = 1


def compact_lists(pairs_ref, counts_ref, lists_ref, kind, blocks, tiles_blk):
    most = pairs_ref.shape[3]
    width = lists_ref.shape[1]
    kinds = blocks // SPLITS
    tiles = blocks * tiles_blk
    f32, bf16 = jnp.float32, jnp.bfloat16
    slot = lax.broadcasted_iota(jnp.int32, (1, most), 1)
    before = lax.broadcasted_iota(jnp.int32, (most, most), 0) < lax.broadcasted_iota(jnp.int32, (most, most), 1)
    before = jnp.where(before, 1.0, 0.0).astype(bf16)
    spot = lax.broadcasted_iota(jnp.int32, (width, most), 0).astype(f32)
    line = lax.broadcasted_iota(jnp.int32, (8, most), 0)
    start = jnp.full((1, 1), UNROLL, f32)
    found = jnp.zeros((8, width), f32)
    for block in range(blocks):
        row = pairs_ref[block, 0] + block * tiles_blk
        keep = jnp.logical_and(slot < counts_ref[block], row % kinds == kind)
        flag = jnp.where(keep, 1.0, 0.0)
        flags = jnp.broadcast_to(flag, (8, most))
        rank = jnp.dot(flags.astype(bf16), before, preferred_element_type=f32)[0:1] + start
        hits = jnp.where(keep, jnp.where(spot == rank, 1.0, 0.0), 0.0).astype(bf16)
        held, across = (row // kinds).astype(f32), pairs_ref[block, 1].astype(f32)
        values = jnp.where(line == 0, held, jnp.where(line == 1, across, 1.0)).astype(bf16)
        found += lax.dot_general(values, hits, (((1,), (1,)), ((), ())), preferred_element_type=f32)
        start = start + jnp.sum(flag, axis=1, keepdims=True)
    index = lax.broadcasted_iota(jnp.int32, (8, width), 0)
    other = jnp.where(found[2:3] > 0.0, found[1:2], float(tiles))
    table = jnp.where(index == 0, found[0:1], jnp.where(index == 1, other, start - UNROLL))
    lists_ref[...] = table.astype(jnp.int32)


def gather_kernel(counts, x_ref, prog_ref, pot_ref, pair_ref, count_ref,
                  xrec_ref, y_ref, yt_ref, sq_ref, pack_ref, pown_ref, lists_ref,
                  xs, own_x, pots, pairs, pair_counts, xbuild, ybuild,
                  send_sem, recv_sem, mate_send, mate_recv, local_sem):
    n_sec, blocks = counts
    sec, blk = lax.axis_index("sec"), lax.axis_index("blk")
    feat, cells_blk = x_ref.shape
    depth = depth_of(feat)
    aux = depth - 8
    gain = gain_of(feat)
    tiles_blk = cells_blk // TILE
    tiles = tiles_blk * blocks
    held_blk = tiles_blk * SPLITS // blocks
    piece = held_blk * WIDTH
    has_to, has_from = sec > 0, sec < n_sec - 1
    core, across, corner = mates = mates_of(blk, blocks)

    def prog_piece(owner, place):
        return prog_ref.at[:, pl.ds(pl.multiple_of(lane_of(owner, place, blocks), WIDTH), WIDTH)]

    moves = [(pot_ref, pots.at[blk]), (pair_ref, pairs.at[blk]), (count_ref, pair_counts.at[blk])]
    for place in range(held_blk):
        start = pl.multiple_of(lane_of(blk, place, blocks), WIDTH)
        moves.append((x_ref.at[:, pl.ds(start, WIDTH)], own_x.at[blk, place]))
    for place in range(held_blk):
        for owner, buffer, start in (
            (blk, pown_ref, 0), (core, pown_ref, piece), (across, pack_ref, cells_blk), (corner, pack_ref, cells_blk + piece)
        ):
            start += place * WIDTH
            moves.append((prog_piece(owner, place), buffer.at[:, start : start + WIDTH]))
    locals_ = [pltpu.make_async_copy(src, dst, local_sem.at[n]) for n, (src, dst) in enumerate(moves)]
    for copy in locals_:
        copy.start()
    greet(
        [(has_to, sec - 1, blk), (has_from, sec + 1, blk)] + [(sec >= 0, sec, mate) for mate in mates]
    )
    sems, mate_sems = (send_sem, recv_sem), (mate_send, mate_recv)
    feat_step = cells_blk // FEAT_CHUNKS
    chunks = [(n * feat_step, feat_step) for n in range(FEAT_CHUNKS)]
    last = 4 * len(chunks)

    def first(c):
        start, size = chunks[c]
        return send(
            x_ref.at[:, start : start + size], xs.at[blk, c], sems, 4 * c, sec - 1, blk
        )

    def first_programs():
        return send(prog_ref, pack_ref.at[:, 0:cells_blk], sems, last, sec - 1, blk)

    def share(c, kind):
        slot = xs.at[across if kind == 2 else blk, c]
        return send(slot, slot, sems, 4 * c + 1 + kind, sec, across if kind == 0 else core)

    def to_mate(k):
        mate = mates[k]
        copies = [(pot_ref, pots.at[blk]), (pair_ref, pairs.at[blk]), (count_ref, pair_counts.at[blk])]
        for place in range(held_blk):
            start = pl.multiple_of(lane_of(mate, place, blocks), WIDTH)
            copies.append((x_ref.at[:, pl.ds(start, WIDTH)], own_x.at[blk, place]))
        per = len(copies)
        return [send(src, dst, mate_sems, per * k + n, sec, mate) for n, (src, dst) in enumerate(copies)]

    @pl.when(has_to)
    def _():
        for c in range(len(chunks)):
            first(c).start()
        first_programs().start()

    to_mates = [to_mate(k) for k in range(3)]
    for n in range(len(to_mates[0])):
        for k in (1, 2, 0):
            to_mates[k][n].start()

    xbuild[...] = jnp.zeros_like(xbuild)
    xbuild[aux:depth, :] = rows_of([1.0] * 3, WIDTH)
    ybuild[...] = jnp.zeros_like(ybuild)
    row = lax.broadcasted_iota(jnp.int32, y_ref.shape[1:], 0)
    y_ref[tiles] = jnp.where(row == aux, NEG, 0.0).astype(jnp.bfloat16)
    lane = lax.broadcasted_iota(jnp.int32, yt_ref.shape[1:], 1)
    yt_ref[tiles] = jnp.where(lane == aux, NEG, 0.0).astype(jnp.bfloat16)
    for copy in locals_:
        copy.wait()

    def build_own(owner):
        for place in range(held_blk):
            cells = own_x[owner, place].astype(jnp.float32)
            scaled = cells * gain
            high = scaled.astype(jnp.bfloat16).astype(jnp.float32)
            xbuild[0:feat, :] = high
            xbuild[depth : depth + feat, :] = scaled - high
            xrec_ref[owner * held_blk + place] = xbuild[...].astype(jnp.bfloat16)
            sq_ref[owner, place : place + 1, :] = sum_squares(cells)

    ones = jnp.ones((1, TILE), jnp.float32)

    def build_next(owner, c):
        begin, size = chunks[c]
        for start in range(begin, begin + size, TILE):
            tile = owner * tiles_blk + start // TILE
            cells = xs[owner, c, :, start - begin : start - begin + TILE].astype(jnp.float32)
            pot = pots[owner, :, start : start + TILE].astype(jnp.float32)
            bias = pot * (LOG2E / EPSILON) - sum_squares(cells) * (gain * 0.5)
            ybuild[0:feat, :] = cells
            ybuild[depth : depth + feat, :] = cells
            ybuild[aux:depth, :] = rows_of(split3(bias) + (ones,) * 3, TILE)
            y_ref[tile] = ybuild[...].astype(jnp.bfloat16)
            yt_ref[tile] = ybuild[...].T.astype(jnp.bfloat16)

    for k in range(3):
        for copy in to_mates[k][:3]:
            copy.wait_recv()
    compact_lists(pairs, pair_counts, lists_ref, blk // SPLITS, blocks, tiles_blk)
    build_own(blk)

    @pl.when(has_from)
    def _():
        for turn in range(len(chunks) + LAG + 1):
            if turn < len(chunks):
                first(turn).wait_recv()
                share(turn, 0).start()
                share(turn, 1).start()
                build_next(blk, turn)
            if 0 <= turn - LAG < len(chunks):
                share(turn - LAG, 0).wait_recv()
                share(turn - LAG, 2).start()
                share(turn - LAG, 1).wait_recv()
                build_next(core, turn - LAG)
                build_next(across, turn - LAG)
            if 0 <= turn - LAG - 1 < len(chunks):
                share(turn - LAG - 1, 2).wait_recv()
                build_next(corner, turn - LAG - 1)
        first_programs().wait_recv()

    @pl.when(jnp.logical_not(has_from))
    def _():
        pack_ref[:, 0:cells_blk] = jnp.zeros((pack_ref.shape[0], cells_blk), jnp.bfloat16)

    for k, mate in enumerate(mates):
        for copy in to_mates[k][3:]:
            copy.wait_recv()
        build_own(mate)

    @pl.when(has_to)
    def _():
        for c in range(len(chunks)):
            first(c).wait_send()
        first_programs().wait_send()

    @pl.when(has_from)
    def _():
        for c in range(len(chunks)):
            for kind in range(3):
                share(c, kind).wait_send()

    for k in range(3):
        for copy in to_mates[k]:
            copy.wait_send()


def rounds_of(lists_ref, unroll):
    return (lists_ref[2, 0] + unroll - 1) // unroll


def stats_kernel(dims, lists_ref, xrec_ref, y_ref, yt_ref, sq_ref, rp_ref, xt_out, cl_ref,
                 top_row, sum_row, top_col, sum_col, tops_row, tops_col, *ready):
    feat, blocks, tiles_blk = dims
    tiles = blocks * tiles_blk
    held_blk = tiles_blk * SPLITS // blocks
    held = blocks * held_blk
    half_gain = gain_of(feat) * 0.5
    depth = depth_of(feat)
    aux = depth - 8
    at_end = lax.axis_index("sec") == lax.axis_size("sec") - 1
    rounds = rounds_of(lists_ref, UNROLL)
    for ref in (top_row, top_col):
        ref[...] = jnp.full_like(ref, NEG)
    for ref in (sum_row, sum_col):
        ref[...] = jnp.zeros_like(ref)

    def sweep(scores_of, ready, tops, top_acc, sum_acc, by_row):
        rows, width = ready[0].shape
        size = rows // PARTS

        def make(at, slot):
            best = None
            for start in range(0, rows, size):
                here = pl.ds(start, size)
                scores = scores_of(lists_ref[0, at], lists_ref[1, at], here)
                ready[slot][here, :] = scores
                found = jnp.max(scores.reshape(size // 8, 8, width), axis=0)
                best = found if best is None else jnp.maximum(best, found)
            tops[slot] = best

        def use(at, slot):
            target = lists_ref[0 if by_row else 1, at]
            old = top_acc[target]
            new = jnp.maximum(old, tops[slot])
            total = sum_acc[target] * jnp.exp2(old - new)
            for start in range(0, rows, size):
                scores = ready[slot][start : start + size, :].reshape(size // 8, 8, width)
                total = total + jnp.sum(jnp.exp2(scores - new[None]), axis=0)
            sum_acc[target] = total
            top_acc[target] = new

        for n in range(UNROLL):
            make(UNROLL + n, n)

        def step(index, carry):
            for n in range(UNROLL):
                at = index * UNROLL + UNROLL + n
                use(at, n)
                make(at + UNROLL, n)
            return carry

        lax.fori_loop(0, rounds, step, 0)

    def level_of(tops, sums):
        top = jnp.max(tops, axis=0, keepdims=True)
        total = jnp.sum(sums * jnp.exp2(tops - top), axis=0, keepdims=True)
        return top, total

    sweep(
        lambda row, col, here: jnp.dot(yt_ref[col, here, :], xrec_ref[row], preferred_element_type=jnp.float32),
        ready[:UNROLL], tops_row, top_row, sum_row, True,
    )
    record_row = lax.broadcasted_iota(jnp.int32, (8, WIDTH), 0)
    for row in range(held):
        owner, place = row // held_blk, row % held_blk
        top, total = level_of(top_row[row], sum_row[row])
        level = top + jnp.log2(total)
        potential = (sq_ref[owner, place : place + 1, :] * half_gain - level) * (EPSILON / LOG2E)
        rp_ref[owner, place : place + 1, :] = jnp.where(at_end, 0.0, potential)
        extra = rows_of((1.0,) * 3 + split3(-level), WIDTH)
        record = xrec_ref[row].astype(jnp.float32)
        record = jnp.concatenate([record[0:aux], extra, record[depth:]], axis=0)
        xt_out[row] = record.T.astype(jnp.bfloat16)
    sweep(
        lambda row, col, here: jnp.dot(xt_out[row, here, :], y_ref[col], preferred_element_type=jnp.float32),
        ready[UNROLL:], tops_col, top_col, sum_col, False,
    )
    for col in range(tiles):
        top, total = level_of(top_col[col], sum_col[col])
        cl_ref[col : col + 1, :] = jnp.where(total > 0.0, top + jnp.log2(total), NEG)


def merge_kernel(counts, rp_ref, cl_ref, pack_ref, pown_ref, far_ref, level_ref, home_ref, extra_ref,
                 parts, send_sem, recv_sem):
    n_sec, blocks = counts
    sec, blk = lax.axis_index("sec"), lax.axis_index("blk")
    tiles = cl_ref.shape[0]
    core, across, corner = mates = mates_of(blk, blocks)
    sems = (send_sem, recv_sem)
    greet([(sec >= 0, sec, mate) for mate in mates])
    copies = []
    for k, mate in enumerate(mates):
        copies.append(send(cl_ref, parts.at[blk], sems, 2 * k, sec, mate))
        copies.append(send(rp_ref.at[mate], home_ref.at[blk], sems, 2 * k + 1, sec, mate))
    piece = pown_ref.shape[1] // 2
    cells = pack_ref.shape[1] - 2 * piece
    beside = [
        (pown_ref, piece, piece, 2 * cells), (far_ref, cells + piece, piece, 2 * cells + piece),
        (pack_ref, 0, cells, 0), (far_ref, 0, cells, cells),
    ]
    for n, (ref, start, size, place) in enumerate(beside):
        copies.append(
            send(ref.at[:, start : start + size], extra_ref.at[:, place : place + size], sems, 2 * len(mates) + n, sec, core)
        )
    for k in (1, 2, 0):
        for copy in copies[2 * k : 2 * k + 2]:
            copy.start()
    for copy in copies[2 * len(mates) :]:
        copy.start()
    parts[blk] = cl_ref[...]
    home_ref[blk] = rp_ref[blk]
    level_ref[tiles:, :] = jnp.zeros((level_ref.shape[0] - tiles, TILE), jnp.float32)
    for copy in copies[: 2 * len(mates)]:
        copy.wait_recv()
    levels = [parts[n] for n in range(blocks)]
    top = functools.reduce(jnp.maximum, levels)
    total = functools.reduce(jnp.add, [jnp.exp2(level - top) for level in levels])
    level_ref[0:tiles, :] = top + jnp.log2(total)
    for copy in copies[2 * len(mates) :]:
        copy.wait_recv()
    for copy in copies:
        copy.wait_send()


def plan_kernel(dims, lists_ref, xt_ref, y_ref, level_ref, pack_ref, pown_ref, far_ref, extra_ref, pot_ref, home_ref,
                fnum_ref, fden_ref, bnum_ref, bden_ref, rows_ref, cols_ref,
                acc_row, acc_col, ext_next_ref, ext_own_ref, *ready):
    feat, blocks, tiles_blk = dims
    tiles = blocks * tiles_blk
    held_blk = tiles_blk * SPLITS // blocks
    held = blocks * held_blk
    cells_blk = tiles_blk * TILE
    piece = held_blk * WIDTH
    progs = fnum_ref.shape[1]
    kept = acc_row.shape[1]
    at_end = lax.axis_index("sec") == lax.axis_size("sec") - 1
    blk = lax.axis_index("blk")
    rounds = rounds_of(lists_ref, SLOTS)
    scores, plans = ready[:SLOTS], ready[SLOTS:]

    def make(at, place):
        scores[place][...] = jnp.dot(
            xt_ref[lists_ref[0, at]], y_ref[lists_ref[1, at]], preferred_element_type=jnp.float32
        )

    make(UNROLL, 0)
    plans[1][...] = jnp.zeros_like(plans[1])
    acc_row[...] = jnp.zeros_like(acc_row)
    acc_col[...] = jnp.zeros_like(acc_col)
    ext_next_ref[tiles] = jnp.zeros(ext_next_ref.shape[1:], jnp.bfloat16)
    core, across, corner = mates_of(blk, blocks)
    sources = (
        (blk, pack_ref, 0, pown_ref, 0), (core, extra_ref, 0, extra_ref, 2 * cells_blk),
        (across, far_ref, 0, far_ref, cells_blk), (corner, extra_ref, cells_blk, extra_ref, 2 * cells_blk + piece),
    )
    for owner, nums, begin, owns, shift in sources:
        for tile in range(tiles_blk):
            start = begin + tile * TILE
            ext_next_ref[owner * tiles_blk + tile, 0:progs, :] = nums[:, start : start + TILE]
            ext_next_ref[owner * tiles_blk + tile, progs:, :] = ext_tail(progs, TILE)
        for place in range(held_blk):
            start = shift + place * WIDTH
            ext_own_ref[owner * held_blk + place, 0:progs, :] = owns[:, start : start + WIDTH]
            ext_own_ref[owner * held_blk + place, progs:, :] = ext_tail(progs, WIDTH)
    for owner in range(blocks):
        for place in range(held_blk):
            start = lane_of(owner, place, blocks)
            rows_ref[:, start : start + WIDTH] = home_ref[owner, place : place + 1, :]
    for tile in range(tiles_blk):
        here = slice(tile * TILE, (tile + 1) * TILE)
        level = level_ref[pl.ds(blk * tiles_blk + tile, 1), :]
        potential = pot_ref[:, here].astype(jnp.float32) - level * (EPSILON / LOG2E)
        cols_ref[:, here] = jnp.where(at_end, 0.0, potential)

    def weigh(at, place):
        level = level_ref[pl.ds(lists_ref[1, at], 1), :]
        plans[place][...] = jnp.exp2(scores[place][...] - level).astype(jnp.bfloat16)

    def gather(at, place):
        row, col = lists_ref[0, at], lists_ref[1, at]
        plan = plans[place][...]
        acc_row[row] += lax.dot_general(
            ext_next_ref[col], plan, (((1,), (1,)), ((), ())), preferred_element_type=jnp.float32
        )[0:kept]
        acc_col[col] += jnp.dot(ext_own_ref[row], plan, preferred_element_type=jnp.float32)[0:kept]

    def step(index, carry):
        for n in range(SLOTS):
            at = index * SLOTS + UNROLL + n
            make(at + 1, (n + 1) % SLOTS)
            gather(at - 1, (n + 1) % SLOTS)
            weigh(at, n)
        return carry

    lax.fori_loop(0, rounds, step, 0)
    gather(rounds * SLOTS + UNROLL - 1, SLOTS - 1)
    for row in range(held):
        owner, place = row // held_blk, row % held_blk
        fnum_ref[owner, :, place * WIDTH : (place + 1) * WIDTH] = acc_row[row, 0:progs, :]
        fden_ref[owner, place : place + 1, :] = acc_row[row, progs : progs + 1, :]
    for col in range(tiles):
        owner, place = col // tiles_blk, col % tiles_blk
        bnum_ref[owner, place] = acc_col[col, 0:progs, :]
        bden_ref[owner, place : place + 1, :] = acc_col[col, progs : progs + 1, :]


def finish_kernel(counts, fnum_ref, fden_ref, bnum_ref, bden_ref, out_ref,
                  hn, hd, an, ad, keep, keep_den, go, go_den, bn, bd, ship, ship_den, cn, cd,
                  send_sem, recv_sem):
    n_sec, blocks = counts
    sec, blk = lax.axis_index("sec"), lax.axis_index("blk")
    tiles_blk = bnum_ref.shape[1]
    held_blk = fden_ref.shape[1]
    kinds = blocks // SPLITS
    has_to, has_from = sec < n_sec - 1, sec > 0
    core, across, corner = mates = mates_of(blk, blocks)
    me, side = blk % 2, blk // 2
    sems = (send_sem, recv_sem)
    greet(
        [(has_to, sec + 1, blk), (has_from, sec - 1, blk)] + [(sec >= 0, sec, mate) for mate in mates]
    )

    def homeward(k, n):
        mate = mates[k]
        src, dst = ((fnum_ref, hn), (fden_ref, hd))[n]
        return send(src.at[mate], dst.at[blk], sems, 2 * k + n, sec, mate)

    steps = tiles_blk + 1
    base = 6

    def pair(t, far):
        place = 1 - side if far else side
        source = 2 * place + 1 - me
        number = base + 2 * t + (0 if far else 1)
        slot = 0 if far else 1
        if t == tiles_blk:
            return send(bden_ref.at[source], ad.at[slot], sems, number, sec, core)
        return send(bnum_ref.at[source, t], an.at[slot, t], sems, number, sec, core)

    def cross(t):
        number = base + 2 * steps + t
        if t == tiles_blk:
            return send(go_den, bd, sems, number, sec, across)
        return send(go.at[t], bn.at[t], sems, number, sec, across)

    def onward(t):
        number = base + 3 * steps + t
        if t == tiles_blk:
            return send(ship_den, cd, sems, number, sec + 1, blk)
        return send(ship.at[t], cn.at[t], sems, number, sec + 1, blk)

    order = [tiles_blk] + list(range(tiles_blk))

    @pl.when(has_to)
    def _():
        for t in order:
            pair(t, True).start()
        for t in order:
            pair(t, False).start()

    hn[blk] = fnum_ref[blk]
    hd[blk] = fden_ref[blk]
    far, near = 2 * (1 - side) + me, 2 * side + me

    @pl.when(has_to)
    def _():
        for t in order:
            pair(t, True).wait_recv()
            if t == tiles_blk:
                go_den[...] = bden_ref[far] + ad[0]
            else:
                go[t] = (bnum_ref[far, t] + an[0, t]).astype(jnp.bfloat16)
            cross(t).start()

    for k in (1, 2, 0):
        for n in range(2):
            homeward(k, n).start()

    @pl.when(has_to)
    def _():
        for t in order:
            pair(t, False).wait_recv()
            if t == tiles_blk:
                keep_den[...] = bden_ref[near] + ad[1]
            else:
                keep[t] = bnum_ref[near, t] + an[1, t]
        for t in order:
            cross(t).wait_recv()
            if t == tiles_blk:
                ship_den[...] = keep_den[...] + bd[...]
            else:
                ship[t] = (keep[t] + bn[t].astype(jnp.float32)).astype(jnp.bfloat16)
            onward(t).start()

    for k in range(3):
        for n in range(2):
            homeward(k, n).wait_recv()

    @pl.when(jnp.logical_not(has_from))
    def _():
        cn[...] = jnp.zeros_like(cn)
        cd[...] = jnp.zeros_like(cd)

    for t in order:

        @pl.when(has_from)
        def _():
            onward(t).wait_recv()

        if t == tiles_blk:
            continue
        place, kind = t // kinds, t % kinds
        owners = [kind * SPLITS + n for n in range(SPLITS)]
        here = slice(place * WIDTH, (place + 1) * WIDTH)
        for n, owner in enumerate(owners):
            part = slice(n * WIDTH, (n + 1) * WIDTH)
            number = hn[owner, :, here] + cn[t, :, part].astype(jnp.float32)
            weight = hd[owner, place : place + 1, :] + cd[t : t + 1, part]
            start = t * TILE + n * WIDTH
            out_ref[:, start : start + WIDTH] = (number / weight).astype(jnp.bfloat16)

    for k in range(3):
        for n in range(2):
            homeward(k, n).wait_send()

    @pl.when(has_to)
    def _():
        for t in range(steps):
            pair(t, True).wait_send()
            pair(t, False).wait_send()
            cross(t).wait_send()
            onward(t).wait_send()


def exchange(kernel, number, out_shape, operands, scratch, space=pltpu.VMEM):
    outs = jax.tree.map(lambda _: pl.BlockSpec(memory_space=pltpu.VMEM), out_shape)
    return pl.pallas_call(
        kernel, out_shape=out_shape, in_specs=[pl.BlockSpec(memory_space=space)] * len(operands),
        out_specs=outs, scratch_shapes=scratch,
        compiler_params=pltpu.CompilerParams(
            collective_id=number, has_side_effects=True, vmem_limit_bytes=VMEM_LIMIT
        ),
    )(*operands)


def call(kernel, out_shape, operands, scratch):
    outs = jax.tree.map(lambda _: pl.BlockSpec(memory_space=pltpu.VMEM), out_shape)
    return pl.pallas_call(
        kernel, out_shape=out_shape,
        in_specs=[pl.BlockSpec(memory_space=pltpu.SMEM)]
        + [pl.BlockSpec(memory_space=pltpu.VMEM)] * (len(operands) - 1),
        out_specs=outs, scratch_shapes=scratch,
        compiler_params=pltpu.CompilerParams(vmem_limit_bytes=VMEM_LIMIT),
    )(*operands)


def body(features, programs, column_pot, tile_pairs, pair_counts):
    feat, cells_blk = features.shape[1:]
    progs = programs.shape[1]
    tiles_blk = cells_blk // TILE
    most = tile_pairs.shape[2]
    blocks, n_sec = lax.axis_size("blk"), lax.axis_size("sec")
    tiles = tiles_blk * blocks
    held_blk = tiles_blk * SPLITS // blocks
    held = blocks * held_blk
    dims = (feat, blocks, tiles_blk)
    counts = (n_sec, blocks)
    depth, ext = depth_of(feat), ext_of(progs)
    f32, bf16, i32 = jnp.float32, jnp.bfloat16, jnp.int32
    shape, vmem = jax.ShapeDtypeStruct, pltpu.VMEM

    def dma(number):
        return [pltpu.SemaphoreType.DMA((number,))] * 2

    piece = held_blk * WIDTH
    kept = -(-(progs + 1) // 8) * 8
    mate_copies = (blocks - 1) * (held_blk + 3)
    packed = cells_blk + 2 * piece
    spaced = [
        pltpu.with_memory_space_constraint(part, pltpu.HBM)
        for part in (features[0], programs[0], column_pot, tile_pairs)
    ]
    xrec, y, yt, sq, pack, pown, lists = exchange(
        functools.partial(gather_kernel, counts), 0,
        (
            shape((held, 2 * depth, WIDTH), bf16),
            shape((tiles + 1, 2 * depth, TILE), bf16),
            shape((tiles + 1, TILE, 2 * depth), bf16),
            shape((blocks, held_blk, WIDTH), f32),
            shape((progs, packed), bf16),
            shape((progs, 2 * piece), bf16),
            shape((8, lists_width(blocks, most)), i32),
        ),
        (*spaced, pair_counts),
        [
            vmem((blocks, FEAT_CHUNKS, feat, cells_blk // FEAT_CHUNKS), bf16),
            vmem((blocks, held_blk, feat, WIDTH), bf16),
            vmem((blocks, 1, cells_blk), bf16),
            vmem((blocks, 2, 1, most), i32),
            vmem((blocks, 1, 1), i32),
            vmem((2 * depth, WIDTH), f32),
            vmem((2 * depth, TILE), f32),
            *dma(4 * FEAT_CHUNKS + 1), *dma(mate_copies), pltpu.SemaphoreType.DMA((3 + 5 * held_blk,)),
        ],
        pltpu.HBM,
    )
    far = lax.ppermute(pack, "blk", [(source, (source + 2) % blocks) for source in range(blocks)])
    pots = shape((blocks, held_blk, WIDTH), f32)
    tall, wide = vmem((TILE, WIDTH), f32), vmem((WIDTH, TILE), f32)
    rp, xt, cl = call(
        functools.partial(stats_kernel, dims),
        (pots, shape((held, WIDTH, 2 * depth), bf16), shape((tiles, TILE), f32)),
        (lists, xrec, y, yt, sq),
        [
            vmem((held, 8, WIDTH), f32), vmem((held, 8, WIDTH), f32),
            vmem((tiles + 1, 8, TILE), f32), vmem((tiles + 1, 8, TILE), f32),
            vmem((UNROLL, 8, WIDTH), f32), vmem((UNROLL, 8, TILE), f32), *[tall] * UNROLL, *[wide] * UNROLL,
        ],
    )
    level, home, extra = exchange(
        functools.partial(merge_kernel, counts), 1,
        (shape((tiles + 8, TILE), f32), pots, shape((progs, 2 * (cells_blk + piece)), bf16)), (rp, cl, pack, pown, far),
        [vmem((blocks, tiles, TILE), f32), *dma(2 * (blocks - 1) + 4)],
    )
    line = shape((1, cells_blk), f32)
    flat = vmem((WIDTH, TILE), bf16)
    fnum, fden, bnum, bden, row_out, col_out = call(
        functools.partial(plan_kernel, dims),
        (
            shape((blocks, progs, held_blk * WIDTH), f32), pots,
            shape((blocks, tiles_blk, progs, TILE), f32), shape((blocks, tiles_blk, TILE), f32), line, line,
        ),
        (lists, xt, y, level, pack, pown, far, extra, column_pot, home),
        [
            vmem((held, kept, WIDTH), f32), vmem((tiles + 1, kept, TILE), f32),
            vmem((tiles + 1, ext, TILE), bf16), vmem((held, ext, WIDTH), bf16), *[wide] * SLOTS, *[flat] * SLOTS,
        ],
    )
    num, den = vmem((tiles_blk, progs, TILE), bf16), vmem((tiles_blk, TILE), f32)
    smoothed = exchange(
        functools.partial(finish_kernel, counts), 2, shape((progs, cells_blk), bf16), (fnum, fden, bnum, bden),
        [
            vmem((blocks, progs, held_blk * WIDTH), f32), vmem((blocks, held_blk, WIDTH), f32),
            vmem((2, tiles_blk, progs, TILE), f32), vmem((2, tiles_blk, TILE), f32),
            vmem((tiles_blk, progs, TILE), f32), den, num, den, num, den, num, den, num, den,
            *dma(6 + 4 * (tiles_blk + 1)),
        ],
    )
    return smoothed[None], row_out, col_out


def solution(mesh):
    in_specs = (
        P("sec", None, "blk"),
        P("sec", None, "blk"),
        P("sec", "blk"),
        P(None, "sec", "blk"),
        P("sec", "blk"),
    )
    out_specs = (P("sec", None, "blk"), P("sec", "blk"), P("sec", "blk"))
    return jax.shard_map(body, mesh=mesh, in_specs=in_specs, out_specs=out_specs, check_vma=False)
```

```python
import functools
import math

import jax
import jax.numpy as jnp
from jax import lax
from jax.experimental import pallas as pl
from jax.experimental.pallas import tpu as pltpu
from jax.sharding import PartitionSpec as P

TILE = 512
EPSILON = 0.05
LOG2E = math.log2(math.e)
NEG = -1e30
UNROLL = 4
SLOTS = 2
SPLITS = 2
WIDTH = TILE // SPLITS
LANES = 128
VMEM_LIMIT = 24 << 20
MESH = pl.DeviceIdType.MESH


def depth_of(feat):
    return -(-(feat + 8) // 16) * 16


def ext_of(progs):
    return -(-(progs + 1) // 16) * 16


def gain_of(feat):
    return 2.0 * LOG2E / (feat * EPSILON)


def split3(value):
    hi = value.astype(jnp.bfloat16).astype(jnp.float32)
    rest = value - hi
    mid = rest.astype(jnp.bfloat16).astype(jnp.float32)
    return hi, mid, rest - mid


def lists_width(blocks, most):
    return -(-(blocks * most + 3 * UNROLL) // LANES) * LANES


def rows_of(pieces, width):
    index = lax.broadcasted_iota(jnp.int32, (8, width), 0)
    block = jnp.zeros((8, width), jnp.float32)
    for place, piece in enumerate(pieces):
        block = jnp.where(index == place, piece, block)
    return block


def sum_squares(cells):
    return jnp.sum(cells * cells, axis=0, keepdims=True)


def lane_of(owner, place, blocks):
    kinds = blocks // SPLITS
    return (place * kinds + owner // SPLITS) * TILE + (owner % SPLITS) * WIDTH


def greet(targets):
    barrier = pltpu.get_barrier_semaphore()
    expected = jnp.int32(0)
    for used, sec, blk in targets:

        @pl.when(used)
        def _():
            pl.semaphore_signal(barrier, inc=1, device_id=(sec, blk), device_id_type=MESH)

        expected = expected + jnp.where(used, 1, 0)
    pl.semaphore_wait(barrier, expected)


def send(src, dst, sems, place, sec, blk):
    return pltpu.make_async_remote_copy(
        src_ref=src, dst_ref=dst, send_sem=sems[0].at[place], recv_sem=sems[1].at[place],
        device_id=(sec, blk), device_id_type=MESH,
    )


def mates_of(blk, blocks):
    core = blk + 1 - 2 * (blk % 2)
    across = (blk + 2) % blocks
    corner = core + 2 - 4 * (core // 2)
    return core, across, corner


def ext_tail(progs, width):
    index = lax.broadcasted_iota(jnp.int32, (ext_of(progs) - progs, width), 0)
    return jnp.where(index == 0, 1.0, 0.0).astype(jnp.bfloat16)


FEAT_CHUNKS = 4
LAG = 3
PARTS = 1


def compact_lists(pairs_ref, counts_ref, lists_ref, kind, blocks, tiles_blk):
    most = pairs_ref.shape[3]
    width = lists_ref.shape[1]
    kinds = blocks // SPLITS
    tiles = blocks * tiles_blk
    f32, bf16 = jnp.float32, jnp.bfloat16
    slot = lax.broadcasted_iota(jnp.int32, (1, most), 1)
    before = lax.broadcasted_iota(jnp.int32, (most, most), 0) < lax.broadcasted_iota(jnp.int32, (most, most), 1)
    before = jnp.where(before, 1.0, 0.0).astype(bf16)
    spot = lax.broadcasted_iota(jnp.int32, (width, most), 0).astype(f32)
    line = lax.broadcasted_iota(jnp.int32, (8, most), 0)
    start = jnp.full((1, 1), UNROLL, f32)
    found = jnp.zeros((8, width), f32)
    for block in range(blocks):
        row = pairs_ref[block, 0] + block * tiles_blk
        keep = jnp.logical_and(slot < counts_ref[block], row % kinds == kind)
        flag = jnp.where(keep, 1.0, 0.0)
        flags = jnp.broadcast_to(flag, (8, most))
        rank = jnp.dot(flags.astype(bf16), before, preferred_element_type=f32)[0:1] + start
        hits = jnp.where(keep, jnp.where(spot == rank, 1.0, 0.0), 0.0).astype(bf16)
        held, across = (row // kinds).astype(f32), pairs_ref[block, 1].astype(f32)
        values = jnp.where(line == 0, held, jnp.where(line == 1, across, 1.0)).astype(bf16)
        found += lax.dot_general(values, hits, (((1,), (1,)), ((), ())), preferred_element_type=f32)
        start = start + jnp.sum(flag, axis=1, keepdims=True)
    index = lax.broadcasted_iota(jnp.int32, (8, width), 0)
    other = jnp.where(found[2:3] > 0.0, found[1:2], float(tiles))
    table = jnp.where(index == 0, found[0:1], jnp.where(index == 1, other, start - UNROLL))
    lists_ref[...] = table.astype(jnp.int32)


def gather_kernel(counts, x_ref, prog_ref, pot_ref, pair_ref, count_ref,
                  xrec_ref, y_ref, yt_ref, sq_ref, pack_ref, pown_ref, lists_ref,
                  xs, own_x, pots, pairs, pair_counts, xbuild, ybuild,
                  send_sem, recv_sem, mate_send, mate_recv, local_sem):
    n_sec, blocks = counts
    sec, blk = lax.axis_index("sec"), lax.axis_index("blk")
    feat, cells_blk = x_ref.shape
    depth = depth_of(feat)
    aux = depth - 8
    gain = gain_of(feat)
    tiles_blk = cells_blk // TILE
    tiles = tiles_blk * blocks
    held_blk = tiles_blk * SPLITS // blocks
    piece = held_blk * WIDTH
    has_to, has_from = sec > 0, sec < n_sec - 1
    core, across, corner = mates = mates_of(blk, blocks)

    def prog_piece(owner, place):
        return prog_ref.at[:, pl.ds(pl.multiple_of(lane_of(owner, place, blocks), WIDTH), WIDTH)]

    moves = [(pot_ref, pots.at[blk]), (pair_ref, pairs.at[blk]), (count_ref, pair_counts.at[blk])]
    for place in range(held_blk):
        start = pl.multiple_of(lane_of(blk, place, blocks), WIDTH)
        moves.append((x_ref.at[:, pl.ds(start, WIDTH)], own_x.at[blk, place]))
    for place in range(held_blk):
        for owner, buffer, start in (
            (blk, pown_ref, 0), (core, pown_ref, piece), (across, pack_ref, cells_blk), (corner, pack_ref, cells_blk + piece)
        ):
            start += place * WIDTH
            moves.append((prog_piece(owner, place), buffer.at[:, start : start + WIDTH]))
    locals_ = [pltpu.make_async_copy(src, dst, local_sem.at[n]) for n, (src, dst) in enumerate(moves)]
    for copy in locals_:
        copy.start()
    greet(
        [(has_to, sec - 1, blk), (has_from, sec + 1, blk)] + [(sec >= 0, sec, mate) for mate in mates]
    )
    sems, mate_sems = (send_sem, recv_sem), (mate_send, mate_recv)
    feat_step = cells_blk // FEAT_CHUNKS
    chunks = [(n * feat_step, feat_step) for n in range(FEAT_CHUNKS)]
    last = 4 * len(chunks)

    def first(c):
        start, size = chunks[c]
        return send(
            x_ref.at[:, start : start + size], xs.at[blk, c], sems, 4 * c, sec - 1, blk
        )

    def first_programs():
        return send(prog_ref, pack_ref.at[:, 0:cells_blk], sems, last, sec - 1, blk)

    def share(c, kind):
        slot = xs.at[across if kind == 2 else blk, c]
        return send(slot, slot, sems, 4 * c + 1 + kind, sec, across if kind == 0 else core)

    def to_mate(k):
        mate = mates[k]
        copies = [(pot_ref, pots.at[blk]), (pair_ref, pairs.at[blk]), (count_ref, pair_counts.at[blk])]
        for place in range(held_blk):
            start = pl.multiple_of(lane_of(mate, place, blocks), WIDTH)
            copies.append((x_ref.at[:, pl.ds(start, WIDTH)], own_x.at[blk, place]))
        per = len(copies)
        return [send(src, dst, mate_sems, per * k + n, sec, mate) for n, (src, dst) in enumerate(copies)]

    @pl.when(has_to)
    def _():
        for c in range(len(chunks)):
            first(c).start()

    @pl.when(jnp.logical_and(has_to, jnp.logical_not(has_from)))
    def _():
        first_programs().start()

    to_mates = [to_mate(k) for k in range(3)]
    for n in range(len(to_mates[0])):
        for k in (1, 2, 0):
            to_mates[k][n].start()

    xbuild[...] = jnp.zeros_like(xbuild)
    xbuild[aux:depth, :] = rows_of([1.0] * 3, WIDTH)
    ybuild[...] = jnp.zeros_like(ybuild)
    row = lax.broadcasted_iota(jnp.int32, y_ref.shape[1:], 0)
    y_ref[tiles] = jnp.where(row == aux, NEG, 0.0).astype(jnp.bfloat16)
    lane = lax.broadcasted_iota(jnp.int32, yt_ref.shape[1:], 1)
    yt_ref[tiles] = jnp.where(lane == aux, NEG, 0.0).astype(jnp.bfloat16)
    for copy in locals_:
        copy.wait()

    def build_own(owner):
        for place in range(held_blk):
            cells = own_x[owner, place].astype(jnp.float32)
            scaled = cells * gain
            high = scaled.astype(jnp.bfloat16).astype(jnp.float32)
            xbuild[0:feat, :] = high
            xbuild[depth : depth + feat, :] = scaled - high
            xrec_ref[owner * held_blk + place] = xbuild[...].astype(jnp.bfloat16)
            sq_ref[owner, place : place + 1, :] = sum_squares(cells)

    ones = jnp.ones((1, TILE), jnp.float32)

    def build_next(owner, c):
        begin, size = chunks[c]
        for start in range(begin, begin + size, TILE):
            tile = owner * tiles_blk + start // TILE
            cells = xs[owner, c, :, start - begin : start - begin + TILE].astype(jnp.float32)
            pot = pots[owner, :, start : start + TILE].astype(jnp.float32)
            bias = pot * (LOG2E / EPSILON) - sum_squares(cells) * (gain * 0.5)
            ybuild[0:feat, :] = cells
            ybuild[depth : depth + feat, :] = cells
            ybuild[aux:depth, :] = rows_of(split3(bias) + (ones,) * 3, TILE)
            y_ref[tile] = ybuild[...].astype(jnp.bfloat16)
            yt_ref[tile] = ybuild[...].T.astype(jnp.bfloat16)

    for k in range(3):
        for copy in to_mates[k][:3]:
            copy.wait_recv()
    compact_lists(pairs, pair_counts, lists_ref, blk // SPLITS, blocks, tiles_blk)
    build_own(blk)

    @pl.when(has_from)
    def _():
        for turn in range(len(chunks) + LAG + 1):
            if turn < len(chunks):
                first(turn).wait_recv()
                share(turn, 0).start()
                share(turn, 1).start()
                if turn == 1:

                    @pl.when(has_to)
                    def _():
                        first_programs().start()

                build_next(blk, turn)
            if 0 <= turn - LAG < len(chunks):
                share(turn - LAG, 0).wait_recv()
                share(turn - LAG, 2).start()
                share(turn - LAG, 1).wait_recv()
                build_next(core, turn - LAG)
                build_next(across, turn - LAG)
            if 0 <= turn - LAG - 1 < len(chunks):
                share(turn - LAG - 1, 2).wait_recv()
                build_next(corner, turn - LAG - 1)
        first_programs().wait_recv()

    @pl.when(jnp.logical_not(has_from))
    def _():
        pack_ref[:, 0:cells_blk] = jnp.zeros((pack_ref.shape[0], cells_blk), jnp.bfloat16)

    for k, mate in enumerate(mates):
        for copy in to_mates[k][3:]:
            copy.wait_recv()
        build_own(mate)

    @pl.when(has_to)
    def _():
        for c in range(len(chunks)):
            first(c).wait_send()
        first_programs().wait_send()

    @pl.when(has_from)
    def _():
        for c in range(len(chunks)):
            for kind in range(3):
                share(c, kind).wait_send()

    for k in range(3):
        for copy in to_mates[k]:
            copy.wait_send()


def rounds_of(lists_ref, unroll):
    return (lists_ref[2, 0] + unroll - 1) // unroll


def stats_kernel(dims, lists_ref, xrec_ref, y_ref, yt_ref, sq_ref, rp_ref, xt_out, cl_ref,
                 top_row, sum_row, top_col, sum_col, tops_row, tops_col, *ready):
    feat, blocks, tiles_blk = dims
    tiles = blocks * tiles_blk
    held_blk = tiles_blk * SPLITS // blocks
    held = blocks * held_blk
    half_gain = gain_of(feat) * 0.5
    depth = depth_of(feat)
    aux = depth - 8
    at_end = lax.axis_index("sec") == lax.axis_size("sec") - 1
    rounds = rounds_of(lists_ref, UNROLL)
    for ref in (top_row, top_col):
        ref[...] = jnp.full_like(ref, NEG)
    for ref in (sum_row, sum_col):
        ref[...] = jnp.zeros_like(ref)

    def sweep(scores_of, ready, tops, top_acc, sum_acc, by_row):
        rows, width = ready[0].shape
        size = rows // PARTS

        def make(at, slot):
            best = None
            for start in range(0, rows, size):
                here = pl.ds(start, size)
                scores = scores_of(lists_ref[0, at], lists_ref[1, at], here)
                ready[slot][here, :] = scores
                found = jnp.max(scores.reshape(size // 8, 8, width), axis=0)
                best = found if best is None else jnp.maximum(best, found)
            tops[slot] = best

        def use(at, slot):
            target = lists_ref[0 if by_row else 1, at]
            old = top_acc[target]
            new = jnp.maximum(old, tops[slot])
            total = sum_acc[target] * jnp.exp2(old - new)
            for start in range(0, rows, size):
                scores = ready[slot][start : start + size, :].reshape(size // 8, 8, width)
                total = total + jnp.sum(jnp.exp2(scores - new[None]), axis=0)
            sum_acc[target] = total
            top_acc[target] = new

        for n in range(UNROLL):
            make(UNROLL + n, n)

        def step(index, carry):
            for n in range(UNROLL):
                at = index * UNROLL + UNROLL + n
                use(at, n)
                make(at + UNROLL, n)
            return carry

        lax.fori_loop(0, rounds, step, 0)

    def level_of(tops, sums):
        top = jnp.max(tops, axis=0, keepdims=True)
        total = jnp.sum(sums * jnp.exp2(tops - top), axis=0, keepdims=True)
        return top, total

    sweep(
        lambda row, col, here: jnp.dot(yt_ref[col, here, :], xrec_ref[row], preferred_element_type=jnp.float32),
        ready[:UNROLL], tops_row, top_row, sum_row, True,
    )
    record_row = lax.broadcasted_iota(jnp.int32, (8, WIDTH), 0)
    for row in range(held):
        owner, place = row // held_blk, row % held_blk
        top, total = level_of(top_row[row], sum_row[row])
        level = top + jnp.log2(total)
        potential = (sq_ref[owner, place : place + 1, :] * half_gain - level) * (EPSILON / LOG2E)
        rp_ref[owner, place : place + 1, :] = jnp.where(at_end, 0.0, potential)
        extra = rows_of((1.0,) * 3 + split3(-level), WIDTH)
        record = xrec_ref[row].astype(jnp.float32)
        record = jnp.concatenate([record[0:aux], extra, record[depth:]], axis=0)
        xt_out[row] = record.T.astype(jnp.bfloat16)
    sweep(
        lambda row, col, here: jnp.dot(xt_out[row, here, :], y_ref[col], preferred_element_type=jnp.float32),
        ready[UNROLL:], tops_col, top_col, sum_col, False,
    )
    for col in range(tiles):
        top, total = level_of(top_col[col], sum_col[col])
        cl_ref[col : col + 1, :] = jnp.where(total > 0.0, top + jnp.log2(total), NEG)


def merge_kernel(counts, rp_ref, cl_ref, pack_ref, pown_ref, far_ref, level_ref, home_ref, extra_ref,
                 parts, send_sem, recv_sem):
    n_sec, blocks = counts
    sec, blk = lax.axis_index("sec"), lax.axis_index("blk")
    tiles = cl_ref.shape[0]
    core, across, corner = mates = mates_of(blk, blocks)
    sems = (send_sem, recv_sem)
    greet([(sec >= 0, sec, mate) for mate in mates])
    copies = []
    for k, mate in enumerate(mates):
        copies.append(send(cl_ref, parts.at[blk], sems, 2 * k, sec, mate))
        copies.append(send(rp_ref.at[mate], home_ref.at[blk], sems, 2 * k + 1, sec, mate))
    piece = pown_ref.shape[1] // 2
    cells = pack_ref.shape[1] - 2 * piece
    beside = [
        (pown_ref, piece, piece, 2 * cells), (far_ref, cells + piece, piece, 2 * cells + piece),
        (pack_ref, 0, cells, 0), (far_ref, 0, cells, cells),
    ]
    for n, (ref, start, size, place) in enumerate(beside):
        copies.append(
            send(ref.at[:, start : start + size], extra_ref.at[:, place : place + size], sems, 2 * len(mates) + n, sec, core)
        )
    for k in (1, 2, 0):
        for copy in copies[2 * k : 2 * k + 2]:
            copy.start()
    for copy in copies[2 * len(mates) :]:
        copy.start()
    parts[blk] = cl_ref[...]
    home_ref[blk] = rp_ref[blk]
    level_ref[tiles:, :] = jnp.zeros((level_ref.shape[0] - tiles, TILE), jnp.float32)
    for copy in copies[: 2 * len(mates)]:
        copy.wait_recv()
    levels = [parts[n] for n in range(blocks)]
    top = functools.reduce(jnp.maximum, levels)
    total = functools.reduce(jnp.add, [jnp.exp2(level - top) for level in levels])
    level_ref[0:tiles, :] = top + jnp.log2(total)
    for copy in copies[2 * len(mates) :]:
        copy.wait_recv()
    for copy in copies:
        copy.wait_send()


def plan_kernel(dims, lists_ref, xt_ref, y_ref, level_ref, pack_ref, pown_ref, far_ref, extra_ref, pot_ref, home_ref,
                fnum_ref, fden_ref, bnum_ref, bden_ref, rows_ref, cols_ref,
                acc_row, acc_col, ext_next_ref, ext_own_ref, *ready):
    feat, blocks, tiles_blk = dims
    tiles = blocks * tiles_blk
    held_blk = tiles_blk * SPLITS // blocks
    held = blocks * held_blk
    cells_blk = tiles_blk * TILE
    piece = held_blk * WIDTH
    progs = fnum_ref.shape[1]
    kept = acc_row.shape[1]
    at_end = lax.axis_index("sec") == lax.axis_size("sec") - 1
    blk = lax.axis_index("blk")
    rounds = rounds_of(lists_ref, SLOTS)
    scores, plans = ready[:SLOTS], ready[SLOTS:]

    def make(at, place):
        scores[place][...] = jnp.dot(
            xt_ref[lists_ref[0, at]], y_ref[lists_ref[1, at]], preferred_element_type=jnp.float32
        )

    make(UNROLL, 0)
    plans[1][...] = jnp.zeros_like(plans[1])
    acc_row[...] = jnp.zeros_like(acc_row)
    acc_col[...] = jnp.zeros_like(acc_col)
    ext_next_ref[tiles] = jnp.zeros(ext_next_ref.shape[1:], jnp.bfloat16)
    core, across, corner = mates_of(blk, blocks)
    sources = (
        (blk, pack_ref, 0, pown_ref, 0), (core, extra_ref, 0, extra_ref, 2 * cells_blk),
        (across, far_ref, 0, far_ref, cells_blk), (corner, extra_ref, cells_blk, extra_ref, 2 * cells_blk + piece),
    )
    for owner, nums, begin, owns, shift in sources:
        for tile in range(tiles_blk):
            start = begin + tile * TILE
            ext_next_ref[owner * tiles_blk + tile, 0:progs, :] = nums[:, start : start + TILE]
            ext_next_ref[owner * tiles_blk + tile, progs:, :] = ext_tail(progs, TILE)
        for place in range(held_blk):
            start = shift + place * WIDTH
            ext_own_ref[owner * held_blk + place, 0:progs, :] = owns[:, start : start + WIDTH]
            ext_own_ref[owner * held_blk + place, progs:, :] = ext_tail(progs, WIDTH)
    for owner in range(blocks):
        for place in range(held_blk):
            start = lane_of(owner, place, blocks)
            rows_ref[:, start : start + WIDTH] = home_ref[owner, place : place + 1, :]
    for tile in range(tiles_blk):
        here = slice(tile * TILE, (tile + 1) * TILE)
        level = level_ref[pl.ds(blk * tiles_blk + tile, 1), :]
        potential = pot_ref[:, here].astype(jnp.float32) - level * (EPSILON / LOG2E)
        cols_ref[:, here] = jnp.where(at_end, 0.0, potential)

    def weigh(at, place):
        level = level_ref[pl.ds(lists_ref[1, at], 1), :]
        plans[place][...] = jnp.exp2(scores[place][...] - level).astype(jnp.bfloat16)

    def gather(at, place):
        row, col = lists_ref[0, at], lists_ref[1, at]
        plan = plans[place][...]
        acc_row[row] += lax.dot_general(
            ext_next_ref[col], plan, (((1,), (1,)), ((), ())), preferred_element_type=jnp.float32
        )[0:kept]
        acc_col[col] += jnp.dot(ext_own_ref[row], plan, preferred_element_type=jnp.float32)[0:kept]

    def step(index, carry):
        for n in range(SLOTS):
            at = index * SLOTS + UNROLL + n
            make(at + 1, (n + 1) % SLOTS)
            gather(at - 1, (n + 1) % SLOTS)
            weigh(at, n)
        return carry

    lax.fori_loop(0, rounds, step, 0)
    gather(rounds * SLOTS + UNROLL - 1, SLOTS - 1)
    for row in range(held):
        owner, place = row // held_blk, row % held_blk
        fnum_ref[owner, :, place * WIDTH : (place + 1) * WIDTH] = acc_row[row, 0:progs, :]
        fden_ref[owner, place : place + 1, :] = acc_row[row, progs : progs + 1, :]
    for col in range(tiles):
        owner, place = col // tiles_blk, col % tiles_blk
        bnum_ref[owner, place] = acc_col[col, 0:progs, :]
        bden_ref[owner, place : place + 1, :] = acc_col[col, progs : progs + 1, :]


def finish_kernel(counts, fnum_ref, fden_ref, bnum_ref, bden_ref, out_ref,
                  hn, hd, an, ad, keep, keep_den, go, go_den, bn, bd, ship, ship_den, cn, cd,
                  send_sem, recv_sem):
    n_sec, blocks = counts
    sec, blk = lax.axis_index("sec"), lax.axis_index("blk")
    tiles_blk = bnum_ref.shape[1]
    held_blk = fden_ref.shape[1]
    kinds = blocks // SPLITS
    has_to, has_from = sec < n_sec - 1, sec > 0
    core, across, corner = mates = mates_of(blk, blocks)
    me, side = blk % 2, blk // 2
    sems = (send_sem, recv_sem)
    greet(
        [(has_to, sec + 1, blk), (has_from, sec - 1, blk)] + [(sec >= 0, sec, mate) for mate in mates]
    )

    def homeward(k, n):
        mate = mates[k]
        src, dst = ((fnum_ref, hn), (fden_ref, hd))[n]
        return send(src.at[mate], dst.at[blk], sems, 2 * k + n, sec, mate)

    steps = tiles_blk + 1
    base = 6

    def pair(t, far):
        place = 1 - side if far else side
        source = 2 * place + 1 - me
        number = base + 2 * t + (0 if far else 1)
        slot = 0 if far else 1
        if t == tiles_blk:
            return send(bden_ref.at[source], ad.at[slot], sems, number, sec, core)
        return send(bnum_ref.at[source, t], an.at[slot, t], sems, number, sec, core)

    def cross(t):
        number = base + 2 * steps + t
        if t == tiles_blk:
            return send(go_den, bd, sems, number, sec, across)
        return send(go.at[t], bn.at[t], sems, number, sec, across)

    def onward(t):
        number = base + 3 * steps + t
        if t == tiles_blk:
            return send(ship_den, cd, sems, number, sec + 1, blk)
        return send(ship.at[t], cn.at[t], sems, number, sec + 1, blk)

    order = [tiles_blk] + list(range(tiles_blk))

    @pl.when(has_to)
    def _():
        for t in order:
            pair(t, True).start()
        for t in order:
            pair(t, False).start()

    hn[blk] = fnum_ref[blk]
    hd[blk] = fden_ref[blk]
    far, near = 2 * (1 - side) + me, 2 * side + me

    @pl.when(has_to)
    def _():
        for t in order:
            pair(t, True).wait_recv()
            if t == tiles_blk:
                go_den[...] = bden_ref[far] + ad[0]
            else:
                go[t] = (bnum_ref[far, t] + an[0, t]).astype(jnp.bfloat16)
            cross(t).start()

    for k in (1, 2, 0):
        for n in range(2):
            homeward(k, n).start()

    @pl.when(has_to)
    def _():
        for t in order:
            pair(t, False).wait_recv()
            if t == tiles_blk:
                keep_den[...] = bden_ref[near] + ad[1]
            else:
                keep[t] = bnum_ref[near, t] + an[1, t]
        for t in order:
            cross(t).wait_recv()
            if t == tiles_blk:
                ship_den[...] = keep_den[...] + bd[...]
            else:
                ship[t] = (keep[t] + bn[t].astype(jnp.float32)).astype(jnp.bfloat16)
            onward(t).start()

    for k in range(3):
        for n in range(2):
            homeward(k, n).wait_recv()

    @pl.when(jnp.logical_not(has_from))
    def _():
        cn[...] = jnp.zeros_like(cn)
        cd[...] = jnp.zeros_like(cd)

    for t in order:

        @pl.when(has_from)
        def _():
            onward(t).wait_recv()

        if t == tiles_blk:
            continue
        place, kind = t // kinds, t % kinds
        owners = [kind * SPLITS + n for n in range(SPLITS)]
        here = slice(place * WIDTH, (place + 1) * WIDTH)
        for n, owner in enumerate(owners):
            part = slice(n * WIDTH, (n + 1) * WIDTH)
            number = hn[owner, :, here] + cn[t, :, part].astype(jnp.float32)
            weight = hd[owner, place : place + 1, :] + cd[t : t + 1, part]
            start = t * TILE + n * WIDTH
            out_ref[:, start : start + WIDTH] = (number / weight).astype(jnp.bfloat16)

    for k in range(3):
        for n in range(2):
            homeward(k, n).wait_send()

    @pl.when(has_to)
    def _():
        for t in range(steps):
            pair(t, True).wait_send()
            pair(t, False).wait_send()
            cross(t).wait_send()
            onward(t).wait_send()


def exchange(kernel, number, out_shape, operands, scratch, space=pltpu.VMEM):
    outs = jax.tree.map(lambda _: pl.BlockSpec(memory_space=pltpu.VMEM), out_shape)
    return pl.pallas_call(
        kernel, out_shape=out_shape, in_specs=[pl.BlockSpec(memory_space=space)] * len(operands),
        out_specs=outs, scratch_shapes=scratch,
        compiler_params=pltpu.CompilerParams(
            collective_id=number, has_side_effects=True, vmem_limit_bytes=VMEM_LIMIT
        ),
    )(*operands)


def call(kernel, out_shape, operands, scratch):
    outs = jax.tree.map(lambda _: pl.BlockSpec(memory_space=pltpu.VMEM), out_shape)
    return pl.pallas_call(
        kernel, out_shape=out_shape,
        in_specs=[pl.BlockSpec(memory_space=pltpu.SMEM)]
        + [pl.BlockSpec(memory_space=pltpu.VMEM)] * (len(operands) - 1),
        out_specs=outs, scratch_shapes=scratch,
        compiler_params=pltpu.CompilerParams(vmem_limit_bytes=VMEM_LIMIT),
    )(*operands)


def body(features, programs, column_pot, tile_pairs, pair_counts):
    feat, cells_blk = features.shape[1:]
    progs = programs.shape[1]
    tiles_blk = cells_blk // TILE
    most = tile_pairs.shape[2]
    blocks, n_sec = lax.axis_size("blk"), lax.axis_size("sec")
    tiles = tiles_blk * blocks
    held_blk = tiles_blk * SPLITS // blocks
    held = blocks * held_blk
    dims = (feat, blocks, tiles_blk)
    counts = (n_sec, blocks)
    depth, ext = depth_of(feat), ext_of(progs)
    f32, bf16, i32 = jnp.float32, jnp.bfloat16, jnp.int32
    shape, vmem = jax.ShapeDtypeStruct, pltpu.VMEM

    def dma(number):
        return [pltpu.SemaphoreType.DMA((number,))] * 2

    piece = held_blk * WIDTH
    kept = -(-(progs + 1) // 8) * 8
    mate_copies = (blocks - 1) * (held_blk + 3)
    packed = cells_blk + 2 * piece
    spaced = [
        pltpu.with_memory_space_constraint(part, pltpu.HBM)
        for part in (features[0], programs[0], column_pot, tile_pairs)
    ]
    xrec, y, yt, sq, pack, pown, lists = exchange(
        functools.partial(gather_kernel, counts), 0,
        (
            shape((held, 2 * depth, WIDTH), bf16),
            shape((tiles + 1, 2 * depth, TILE), bf16),
            shape((tiles + 1, TILE, 2 * depth), bf16),
            shape((blocks, held_blk, WIDTH), f32),
            shape((progs, packed), bf16),
            shape((progs, 2 * piece), bf16),
            shape((8, lists_width(blocks, most)), i32),
        ),
        (*spaced, pair_counts),
        [
            vmem((blocks, FEAT_CHUNKS, feat, cells_blk // FEAT_CHUNKS), bf16),
            vmem((blocks, held_blk, feat, WIDTH), bf16),
            vmem((blocks, 1, cells_blk), bf16),
            vmem((blocks, 2, 1, most), i32),
            vmem((blocks, 1, 1), i32),
            vmem((2 * depth, WIDTH), f32),
            vmem((2 * depth, TILE), f32),
            *dma(4 * FEAT_CHUNKS + 1), *dma(mate_copies), pltpu.SemaphoreType.DMA((3 + 5 * held_blk,)),
        ],
        pltpu.HBM,
    )
    far = lax.ppermute(pack, "blk", [(source, (source + 2) % blocks) for source in range(blocks)])
    pots = shape((blocks, held_blk, WIDTH), f32)
    tall, wide = vmem((TILE, WIDTH), f32), vmem((WIDTH, TILE), f32)
    rp, xt, cl = call(
        functools.partial(stats_kernel, dims),
        (pots, shape((held, WIDTH, 2 * depth), bf16), shape((tiles, TILE), f32)),
        (lists, xrec, y, yt, sq),
        [
            vmem((held, 8, WIDTH), f32), vmem((held, 8, WIDTH), f32),
            vmem((tiles + 1, 8, TILE), f32), vmem((tiles + 1, 8, TILE), f32),
            vmem((UNROLL, 8, WIDTH), f32), vmem((UNROLL, 8, TILE), f32), *[tall] * UNROLL, *[wide] * UNROLL,
        ],
    )
    level, home, extra = exchange(
        functools.partial(merge_kernel, counts), 1,
        (shape((tiles + 8, TILE), f32), pots, shape((progs, 2 * (cells_blk + piece)), bf16)), (rp, cl, pack, pown, far),
        [vmem((blocks, tiles, TILE), f32), *dma(2 * (blocks - 1) + 4)],
    )
    line = shape((1, cells_blk), f32)
    flat = vmem((WIDTH, TILE), bf16)
    fnum, fden, bnum, bden, row_out, col_out = call(
        functools.partial(plan_kernel, dims),
        (
            shape((blocks, progs, held_blk * WIDTH), f32), pots,
            shape((blocks, tiles_blk, progs, TILE), f32), shape((blocks, tiles_blk, TILE), f32), line, line,
        ),
        (lists, xt, y, level, pack, pown, far, extra, column_pot, home),
        [
            vmem((held, kept, WIDTH), f32), vmem((tiles + 1, kept, TILE), f32),
            vmem((tiles + 1, ext, TILE), bf16), vmem((held, ext, WIDTH), bf16), *[wide] * SLOTS, *[flat] * SLOTS,
        ],
    )
    num, den = vmem((tiles_blk, progs, TILE), bf16), vmem((tiles_blk, TILE), f32)
    smoothed = exchange(
        functools.partial(finish_kernel, counts), 2, shape((progs, cells_blk), bf16), (fnum, fden, bnum, bden),
        [
            vmem((blocks, progs, held_blk * WIDTH), f32), vmem((blocks, held_blk, WIDTH), f32),
            vmem((2, tiles_blk, progs, TILE), f32), vmem((2, tiles_blk, TILE), f32),
            vmem((tiles_blk, progs, TILE), f32), den, num, den, num, den, num, den, num, den,
            *dma(6 + 4 * (tiles_blk + 1)),
        ],
    )
    return smoothed[None], row_out, col_out


def solution(mesh):
    in_specs = (
        P("sec", None, "blk"),
        P("sec", None, "blk"),
        P("sec", "blk"),
        P(None, "sec", "blk"),
        P("sec", "blk"),
    )
    out_specs = (P("sec", None, "blk"), P("sec", "blk"), P("sec", "blk"))
    return jax.shard_map(body, mesh=mesh, in_specs=in_specs, out_specs=out_specs, check_vma=False)
```
